32 devices in a mesh: lat: 16 (over z, x, core), lon: 2 (over y).
Axes of the slice: x: 2, y: 2, z: 4, core: 2. Of those that a mesh axis runs over, the one named last changes fastest.
Arguments:
- state: bfloat16 [2, 96, 128, 256], P(None, 'lat', 'lon'), may hold values from -6 to 6
- upstream: bfloat16 [2, 96, 128, 256], P(None, 'lat', 'lon'), may hold values from -6 to 6
- first_kernel: bfloat16 [9, 256, 256], replicated, may hold values from -0.125 to 0.125
- second_kernel: bfloat16 [9, 256, 256], replicated, may hold values from -0.125 to 0.125
Outputs:
- output_state: bfloat16 [2, 96, 128, 256], P(None, 'lat', 'lon')
- state_grad: bfloat16 [2, 96, 128, 256], P(None, 'lat', 'lon')
- first_grad: float32 [9, 256, 256], P(None, 'lat', 'lon')
- second_grad: float32 [9, 256, 256], P(None, 'lat', 'lon')
The draws below stay inside these ranges and needn't reach their ends.
All inputs are finite; a program needn't handle non-finite values.
Results may differ from the reference program's by a relative error of at most 0.0033.
Values may be sent and summed in bfloat16 or wider, within the bound.
A program may use at most 64 MiB of HBM per device.

```python
import math
import jax
import jax.numpy as jnp

C = 256
BATCH = 2
H = 96
W = 128


def block_scale(stream_key, dims, cuts, least, high):
    factor_of = 1.0
    for position, blocks in cuts:
        steps = jax.random.uniform(jax.random.fold_in(jax.random.fold_in(stream_key, 6), position), (blocks,), jnp.float32, least / len(cuts), high / len(cuts))
        factor_of = factor_of * jnp.repeat(jnp.exp(steps), dims[position] // blocks).reshape((-1,) + (1,) * (len(dims) - 1 - position))
    return factor_of


def normal_values(key, shape, spread, bound, shards=(), kind=jnp.bfloat16):
    values = jax.random.normal(key, shape, jnp.float32) * spread
    if len(shards) > 0:
        values = block_scale(key, shape, shards, -0.22, 0.18) * values
    return jnp.clip(values, min=-bound, max=bound).astype(kind)


def setup_inputs(seed: int = 0) -> dict:
    key_of = jax.random.split(jax.random.key(seed), 5)
    state = normal_values(key_of[0], (BATCH, H, W, C), 1.0, 6.0, ((1, 16), (2, 2)))
    upstream = normal_values(key_of[1], (BATCH, H, W, C), 1.0, 6.0, ((1, 16), (2, 2)))
    first_kernel = normal_values(key_of[2], (9, C, C), (9 * C) ** -0.5, 0.125)
    second_kernel = normal_values(key_of[3], (9, C, C), (9 * C) ** -0.5, 0.125)
    return dict(state=state, upstream=upstream, first_kernel=first_kernel, second_kernel=second_kernel)


def pad_grid(field):
    wide = jnp.concatenate([field[:, :, -1:], field, field[:, :, :1]], axis=2)
    return jnp.pad(wide, ((0, 0), (1, 1), (0, 0), (0, 0)))

def conv_taps(padded, kernel, flipped):
    batch_size = padded.shape[0]
    band_rows = padded.shape[1] - 2
    band_cols = padded.shape[2] - 2
    width = kernel.shape[1]
    total = jnp.zeros((batch_size * band_rows * band_cols, width), jnp.float32)
    for row_off in range(3):
        for col_off in range(3):
            window = padded[:, row_off:row_off + band_rows, col_off:col_off + band_cols, :].reshape(-1, width)
            if flipped:
                tap_mat = kernel[8 - 3 * row_off - col_off].T
            else:
                tap_mat = kernel[3 * row_off + col_off]
            total = total + jnp.dot(window, tap_mat, preferred_element_type=jnp.float32)
    return total.reshape(batch_size, band_rows, band_cols, width)

def kernel_terms(padded, grad_field):
    band_rows = grad_field.shape[1]
    band_cols = grad_field.shape[2]
    width = grad_field.shape[3]
    flat_grad = grad_field.reshape(-1, width)
    result = []
    for row_off in range(3):
        for col_off in range(3):
            window = padded[:, row_off:row_off + band_rows, col_off:col_off + band_cols, :].reshape(-1, width)
            result.append(jnp.dot(window.T, flat_grad, preferred_element_type=jnp.float32))
    return jnp.stack(result)

def reference(state, upstream, first_kernel, second_kernel):
    scale_factor = 1.0 / math.sqrt(H * W)
    state_pad = pad_grid(state)
    pre = conv_taps(state_pad, first_kernel, False)
    active = jax.nn.silu(pre).astype(jnp.bfloat16)
    active_pad = pad_grid(active)
    second_out = conv_taps(active_pad, second_kernel, False)
    output_state = (state.astype(jnp.float32) + second_out).astype(jnp.bfloat16)
    back_act = conv_taps(pad_grid(upstream), second_kernel, True)
    sigma = jax.nn.sigmoid(pre)
    back_pre = (back_act * sigma * (1.0 + pre * (1.0 - sigma))).astype(jnp.bfloat16)
    state_grad = (upstream.astype(jnp.float32) + conv_taps(pad_grid(back_pre), first_kernel, True)).astype(jnp.bfloat16)
    first_grad = kernel_terms(state_pad, back_pre) * scale_factor
    second_grad = kernel_terms(active_pad, upstream) * scale_factor
    return (output_state, state_grad, first_grad, second_grad)
```

```python
import math

import jax
import jax.numpy as jnp
from jax import lax
from jax.experimental import pallas as pl
from jax.experimental.pallas import tpu as pltpu
from jax.sharding import PartitionSpec as P

F32 = jnp.float32
BF16 = jnp.bfloat16
MESH = pl.DeviceIdType.MESH


def with_halo(array, sides, width, wrap):
    for axis, dim in sides:
        size, length = (lax.axis_size(axis), array.shape[dim])
        up = [(i, (i + 1) % size) for i in range(size if wrap else size - 1)]
        down = [(j, i) for i, j in up]
        last = lax.slice_in_dim(array, length - width, length, axis=dim)
        leading = lax.slice_in_dim(array, 0, width, axis=dim)
        before = lax.ppermute(last, axis, up)
        after = lax.ppermute(leading, axis, down)
        array = jnp.concatenate([before, array, after], axis=dim)
    return array


def pad_cycle(stacked):
    wide = with_halo(stacked, (("lon", 3),), 1, True)
    return with_halo(wide, (("lat", 2),), 1, False)


def conv_taps(padded, kernel, flipped):
    band_rows = padded.shape[1] - 2
    band_cols = padded.shape[2] - 2
    total = jnp.zeros((padded.shape[0], band_rows, band_cols, kernel.shape[2]), F32)
    for row_off in range(3):
        for col_off in range(3):
            window = padded[:, row_off : row_off + band_rows, col_off : col_off + band_cols, :]
            tap = 3 * row_off + col_off
            total = total + jnp.einsum(
                "bijd,cd->bijc" if flipped else "bijc,cd->bijd",
                window,
                kernel[8 - tap if flipped else tap],
                preferred_element_type=F32,
            )
    return total


def kernel_terms(padded, grad_field):
    band_rows = grad_field.shape[1]
    band_cols = grad_field.shape[2]
    result = []
    for row_off in range(3):
        for col_off in range(3):
            window = padded[:, row_off : row_off + band_rows, col_off : col_off + band_cols, :]
            result.append(jnp.einsum("bijc,bijd->cd", window, grad_field, preferred_element_type=F32))
    return jnp.stack(result)


def general_body(state, upstream, first_kernel, second_kernel):
    scale_factor = 1.0 / math.sqrt(
        state.shape[1] * lax.axis_size("lat") * state.shape[2] * lax.axis_size("lon")
    )
    both_pad = pad_cycle(jnp.stack([state, upstream]))
    pre = conv_taps(both_pad[0], first_kernel, False)
    active = jax.nn.silu(pre).astype(BF16)
    back_act = conv_taps(both_pad[1], second_kernel, True)
    sigma = jax.nn.sigmoid(pre)
    back_pre = (back_act * sigma * (1.0 + pre * (1.0 - sigma))).astype(BF16)
    inner_pad = pad_cycle(jnp.stack([active, back_pre]))
    output_state = (state.astype(F32) + conv_taps(inner_pad[0], second_kernel, False)).astype(BF16)
    state_grad = (upstream.astype(F32) + conv_taps(inner_pad[1], first_kernel, True)).astype(BF16)
    summed = []
    for terms in (kernel_terms(both_pad[0], back_pre), kernel_terms(inner_pad[0], upstream)):
        part = lax.psum_scatter(terms, "lat", scatter_dimension=1, tiled=True)
        part = lax.psum_scatter(part, "lon", scatter_dimension=2, tiled=True)
        summed.append(part * scale_factor)
    return (output_state, state_grad, summed[0], summed[1])


def stage_plan(lat_size, chans, lon_first):
    bits = lat_size.bit_length() - 1
    order = [0, "lon", 1] if lon_first else [0, 1, "lon"]
    order += list(range(2, bits))
    plan, length, cols = [], lat_size, chans
    for op in order:
        plan.append((op, length, cols))
        if op == "lon":
            cols //= 2
        else:
            length //= 2
    return plan


def fused_kernel(lat_size, scale, plans, names, *refs):
    r = dict(zip(names, refs))
    z = r["z"]
    batch, padded_rows, cols = z.shape[1], z.shape[2], z.shape[3]
    rows = padded_rows - 2
    chans = z.shape[4] // 3
    mid = slice(chans, 2 * chans)
    n_stage = 2 * padded_rows
    lat, lon = lax.axis_index("lat"), lax.axis_index("lon")
    other_lon = 1 - lon
    bits = lat_size.bit_length() - 1

    def bit_of(k):
        return lax.rem(lax.div(lat, 2**k), 2)

    def partner(k):
        return lat + (1 - 2 * bit_of(k)) * 2**k

    loads = [
        pltpu.make_async_copy(r["state"], z.at[0, :, 1 : rows + 1, :, mid], r["load_sem"].at[0]),
        pltpu.make_async_copy(r["upstream"], z.at[1, :, 1 : rows + 1, :, mid], r["load_sem"].at[1]),
        pltpu.make_async_copy(r["k1"], r["w1"], r["load_sem"].at[2]),
        pltpu.make_async_copy(r["k2"], r["w2"], r["load_sem"].at[3]),
    ]
    for load in loads:
        load.start()

    barrier = pltpu.get_barrier_semaphore()

    def greet(to_lat, to_lon):
        pl.semaphore_signal(barrier, inc=1, device_id=(to_lat, to_lon), device_id_type=MESH)

    greet(lat, other_lon)
    for k in range(1, bits):
        greet(partner(k), lon)

    @pl.when(lat > 0)
    def _():
        greet(lat - 1, lon)
        greet(lat - 1, other_lon)

    @pl.when(lat < lat_size - 1)
    def _():
        greet(lat + 1, lon)
        greet(lat + 1, other_lon)

    beside = jnp.where(lat > 0, 2, 0) + jnp.where(lat < lat_size - 1, 2, 0)
    pl.semaphore_wait(barrier, bits + beside)

    def row_copy(pair, f, up):
        src, dst = (rows, 0) if up else (1, rows + 1)
        return pltpu.make_async_remote_copy(
            src_ref=z.at[2 * pair + f, :, src, :, mid],
            dst_ref=z.at[2 * pair + f, :, dst, :, mid],
            send_sem=r["row_send"].at[pair, f, int(up)],
            recv_sem=r["row_recv"].at[pair, f, int(up)],
            device_id=(lat + 1 if up else lat - 1, lon),
            device_id_type=MESH,
        )

    def col_copy(pair, side, place):
        to_lat = (lat, lat + 1, lat - 1)[place]
        return pltpu.make_async_remote_copy(
            src_ref=r["rim_out"].at[pair, side],
            dst_ref=r["rim_in"].at[pair, side, place],
            send_sem=r["col_send"].at[pair, side, place],
            recv_sem=r["col_recv"].at[pair, side, place],
            device_id=(to_lat, other_lon),
            device_id_type=MESH,
        )

    def both_ways(up_copies, down_copies, what, mirrored):
        @pl.when(lat < lat_size - 1)
        def _():
            for c in down_copies if mirrored else up_copies:
                getattr(c, what)()

        @pl.when(lat > 0)
        def _():
            for c in up_copies if mirrored else down_copies:
                getattr(c, what)()

    def copies(pair):
        ups = [row_copy(pair, f, True) for f in range(2)] + [col_copy(pair, s, 1) for s in range(2)]
        downs = [row_copy(pair, f, False) for f in range(2)] + [col_copy(pair, s, 2) for s in range(2)]
        return ups, downs, [col_copy(pair, s, 0) for s in range(2)]

    def send_halo(pair):
        for f in range(2):
            for side, lo, pick in ((1, 0, 0), (0, cols - 16, 15)):
                for b in range(batch):
                    for i in range(1, rows + 1):
                        block = z[2 * pair + f, b, i, lo : lo + 16, mid].astype(F32)
                        r["rim32"][f, side, 2 * i + b : 2 * i + b + 1, :] = block[pick : pick + 1]
        for f in range(2):
            for side in range(2):
                r["rim_out"][pair, side, f] = r["rim32"][f, side].astype(BF16)
        ups, downs, flats = copies(pair)
        for c in flats:
            c.start()
        both_ways(ups, downs, "start", False)

    def shift_rows(pair, row_list):
        for f in range(2):
            fld = 2 * pair + f
            for b in range(batch):
                for i in row_list:
                    x = z[fld, b, i, :, mid].astype(F32)
                    z[fld, b, i, :, 0:chans] = pltpu.roll(x, 1, 0).astype(BF16)
                    z[fld, b, i, :, 2 * chans :] = pltpu.roll(x, cols - 1, 0).astype(BF16)

    def receive_halo(pair):
        ups, downs, flats = copies(pair)
        for c in flats:
            c.wait_recv()
        both_ways(ups, downs, "wait_recv", True)
        zero_row = jnp.zeros((batch, cols, chans), BF16)

        @pl.when(lat == 0)
        def _():
            for f in range(2):
                z[2 * pair + f, :, 0, :, mid] = zero_row
                for s in range(2):
                    r["rim_in"][pair, s, 1, f] = jnp.zeros((n_stage, chans), BF16)

        @pl.when(lat == lat_size - 1)
        def _():
            for f in range(2):
                z[2 * pair + f, :, rows + 1, :, mid] = zero_row
                for s in range(2):
                    r["rim_in"][pair, s, 2, f] = jnp.zeros((n_stage, chans), BF16)

        at = lax.broadcasted_iota(jnp.int32, (n_stage, chans), 0)
        for f in range(2):
            for s in range(2):
                centre = r["rim_in"][pair, s, 0, f].astype(F32)
                above = pltpu.roll(r["rim_in"][pair, s, 1, f].astype(F32), 4, 0)
                below = pltpu.roll(r["rim_in"][pair, s, 2, f].astype(F32), n_stage - 4, 0)
                r["rim32"][f, s] = jnp.where(at < 2, above, jnp.where(at >= n_stage - 2, below, centre))
        shift_rows(pair, (0, rows + 1))
        first = lax.broadcasted_iota(jnp.int32, (16, chans), 0) == 0
        final = lax.broadcasted_iota(jnp.int32, (16, chans), 0) == 15
        for f in range(2):
            fld = 2 * pair + f
            for b in range(batch):
                for i in range(padded_rows):
                    k = 2 * i + b
                    old = z[fld, b, i, 0:16, 0:chans].astype(F32)
                    z[fld, b, i, 0:16, 0:chans] = jnp.where(first, r["rim32"][f, 0, k : k + 1], old).astype(BF16)
                    old = z[fld, b, i, cols - 16 :, 2 * chans :].astype(F32)
                    z[fld, b, i, cols - 16 :, 2 * chans :] = jnp.where(
                        final, r["rim32"][f, 1, k : k + 1], old
                    ).astype(BF16)

    def finish_halo(pair):
        ups, downs, flats = copies(pair)
        for c in flats:
            c.wait_send()
        both_ways(ups, downs, "wait_send", False)

    def stage_copy(grp, s, p):
        op = plans[grp][s][0]
        to = (lat, other_lon) if op == "lon" else (partner(op), lon)
        return pltpu.make_async_remote_copy(
            src_ref=r[f"send{grp}{s}"].at[p],
            dst_ref=r[f"recv{grp}{s}"].at[p],
            send_sem=r["rs_send"].at[grp, s, p],
            recv_sem=r["rs_recv"].at[grp, s, p],
            device_id=to,
            device_id_type=MESH,
        )

    def half(grp, s, p, mine):
        op, length, width = plans[grp][s]
        keep = r[f"keep{grp}{s}"]
        if op == "lon":
            start = pl.multiple_of((lon if mine else other_lon) * (width // 2), width // 2)
            return keep[p, :, :, :, pl.ds(start, width // 2)]
        which = bit_of(op) if mine else 1 - bit_of(op)
        return keep[p, :, :, which]

    def put(grp, s, p, value):
        keep = r[f"keep{grp}{s}"]
        keep[p] = value.reshape(keep.shape[1:])
        r[f"send{grp}{s}"][p] = half(grp, s, p, False).astype(BF16)
        stage_copy(grp, s, p).start()

    def advance(grp, s, p):
        stage_copy(grp, s, p).wait_recv()
        value = half(grp, s, p, True) + r[f"recv{grp}{s}"][p].astype(F32)
        if s + 1 < len(plans[grp]):
            put(grp, s + 1, p, value)
            return
        value = (value * scale).reshape(3, value.shape[2], value.shape[3])
        e = p
        if grp == 0:
            for f in range(3):
                r["g2"][8 - 3 * e - f] = value[f]
        else:
            r["g1"][3 * e : 3 * e + 3] = value

    def window(fld, e):
        return z[fld, :, e : e + rows].reshape(batch * rows * cols, 3 * chans)

    def conv(fld, w, b):
        total = None
        for e in range(3):
            x = z[fld, b, e : e + rows].reshape(rows * cols, 3 * chans)
            part = jnp.dot(x, w[3 * e : 3 * e + 3].reshape(3 * chans, chans), preferred_element_type=F32)
            total = part if total is None else total + part
        return total

    loads[0].wait()
    loads[1].wait()
    send_halo(0)
    shift_rows(0, range(1, rows + 1))
    loads[2].wait()
    loads[3].wait()
    for t in range(9):
        r["w1t"][8 - t] = r["w1"][t].T
        r["w2t"][8 - t] = r["w2"][t].T
    receive_halo(0)

    for b in range(batch):
        pre = conv(0, r["w1"], b)
        sigma = 1.0 / (1.0 + jnp.exp(-pre))
        active = (pre * sigma).astype(BF16)
        z[2, b, 1 : rows + 1, :, mid] = active.reshape(rows, cols, chans)
        r["slope"][b] = sigma * (1.0 + pre * (1.0 - sigma))
    act = z[2, :, 1 : rows + 1, :, mid].reshape(batch * rows * cols, chans)
    for e in range(3):
        terms = lax.dot_general(act, window(1, e), (((0,), (0,)), ((), ())), preferred_element_type=F32)
        put(0, 0, e, jnp.stack([terms[:, f * chans : (f + 1) * chans] for f in range(3)]))
    for b in range(batch):
        back = (conv(1, r["w2t"], b) * r["slope"][b]).astype(BF16)
        z[3, b, 1 : rows + 1, :, mid] = back.reshape(rows, cols, chans)
    send_halo(1)
    for e in range(3):
        advance(0, 0, e)
    back = z[3, :, 1 : rows + 1, :, mid].reshape(batch * rows * cols, chans)
    for e in range(3):
        terms = lax.dot_general(window(0, e), back, (((0,), (0,)), ((), ())), preferred_element_type=F32)
        put(1, 0, e, terms)
    for e in range(3):
        advance(1, 0, e)
    shift_rows(1, range(1, rows + 1))
    receive_halo(1)
    for e in range(3):
        advance(0, 1, e)
    for b in range(batch):
        total = z[0, b, 1 : rows + 1, :, mid].astype(F32) + conv(2, r["w2"], b).reshape(rows, cols, chans)
        r["out"][b] = total.astype(BF16)
    for e in range(3):
        advance(1, 1, e)
    for b in range(batch):
        total = z[1, b, 1 : rows + 1, :, mid].astype(F32) + conv(3, r["w1t"], b).reshape(rows, cols, chans)
        r["sgrad"][b] = total.astype(BF16)
    for s in range(2, len(plans[0])):
        for grp in range(2):
            for e in range(3):
                advance(grp, s, e)
    for pair in range(2):
        finish_halo(pair)
    for grp in range(2):
        for s in range(len(plans[grp])):
            for e in range(3):
                stage_copy(grp, s, e).wait_send()


def fused_body(state, upstream, first_kernel, second_kernel):
    lat_size, lon_size = lax.axis_size("lat"), lax.axis_size("lon")
    batch, rows, cols, chans = state.shape
    scale = 1.0 / math.sqrt(rows * lat_size * cols * lon_size)
    own = chans // lat_size
    n_stage = 2 * (rows + 2)
    plans = [stage_plan(lat_size, chans, True), stage_plan(lat_size, chans, False)]
    steps = len(plans[0])
    scratch = {
        "z": pltpu.VMEM((4, batch, rows + 2, cols, 3 * chans), BF16),
        "w1": pltpu.VMEM((9, chans, chans), BF16),
        "w2": pltpu.VMEM((9, chans, chans), BF16),
        "w1t": pltpu.VMEM((9, chans, chans), BF16),
        "w2t": pltpu.VMEM((9, chans, chans), BF16),
        "slope": pltpu.VMEM((batch, rows * cols, chans), F32),
        "rim32": pltpu.VMEM((2, 2, n_stage, chans), F32),
        "rim_out": pltpu.VMEM((2, 2, 2, n_stage, chans), BF16),
        "rim_in": pltpu.VMEM((2, 2, 3, 2, n_stage, chans), BF16),
        "load_sem": pltpu.SemaphoreType.DMA((4,)),
        "row_send": pltpu.SemaphoreType.DMA((2, 2, 2)),
        "row_recv": pltpu.SemaphoreType.DMA((2, 2, 2)),
        "col_send": pltpu.SemaphoreType.DMA((2, 2, 3)),
        "col_recv": pltpu.SemaphoreType.DMA((2, 2, 3)),
        "rs_send": pltpu.SemaphoreType.DMA((2, steps, 3)),
        "rs_recv": pltpu.SemaphoreType.DMA((2, steps, 3)),
    }
    for grp in range(2):
        for s, (op, length, width) in enumerate(plans[grp]):
            if op == "lon":
                kept, sent = (3, length, own, width), (3, length, own, width // 2)
            else:
                kept, sent = (3, length // 2, 2, own, width), (3, length // 2, own, width)
            scratch[f"keep{grp}{s}"] = pltpu.VMEM((3,) + kept, F32)
            scratch[f"send{grp}{s}"] = pltpu.VMEM((3,) + sent, BF16)
            scratch[f"recv{grp}{s}"] = pltpu.VMEM((3,) + sent, BF16)
    names = ["state", "upstream", "k1", "k2", "out", "sgrad", "g1", "g2"] + list(scratch)

    def kernel(*refs):
        fused_kernel(lat_size, scale, plans, names, *refs)

    vmem = pl.BlockSpec(memory_space=pltpu.VMEM)
    return pl.pallas_call(
        kernel,
        out_shape=(
            jax.ShapeDtypeStruct(state.shape, BF16),
            jax.ShapeDtypeStruct(state.shape, BF16),
            jax.ShapeDtypeStruct((9, own, chans // 2), F32),
            jax.ShapeDtypeStruct((9, own, chans // 2), F32),
        ),
        in_specs=[pl.BlockSpec(memory_space=pl.ANY)] * 4,
        out_specs=(vmem,) * 4,
        scratch_shapes=list(scratch.values()),
        compiler_params=pltpu.CompilerParams(
            collective_id=0, has_side_effects=True, vmem_limit_bytes=56 * 2**20
        ),
    )(state, upstream, first_kernel, second_kernel)


def body(state, upstream, first_kernel, second_kernel):
    lat_size, lon_size = lax.axis_size("lat"), lax.axis_size("lon")
    batch, rows, cols, chans = state.shape
    fits = (
        lon_size == 2
        and lat_size >= 4
        and lat_size & (lat_size - 1) == 0
        and batch == 2
        and 2 * (rows + 2) == 16
        and cols % 16 == 0
        and chans % (16 * lat_size) == 0
        and (chans // 2) % 128 == 0
    )
    run = fused_body if fits else general_body
    return run(state, upstream, first_kernel, second_kernel)


def solution(mesh):
    placed = (P(None, "lat", "lon", None), P(None, "lat", "lon", None), P(), P())
    return jax.shard_map(
        body,
        mesh=mesh,
        in_specs=placed,
        out_specs=(
            P(None, "lat", "lon", None),
            P(None, "lat", "lon", None),
            P(None, "lat", "lon"),
            P(None, "lat", "lon"),
        ),
        check_vma=False,
    )
```

```python
import math

import jax
import jax.numpy as jnp
from jax import lax
from jax.experimental import pallas as pl
from jax.experimental.pallas import tpu as pltpu
from jax.sharding import PartitionSpec as P

F32 = jnp.float32
BF16 = jnp.bfloat16
MESH = pl.DeviceIdType.MESH


def with_halo(array, sides, width, wrap):
    for axis, dim in sides:
        size, length = (lax.axis_size(axis), array.shape[dim])
        up = [(i, (i + 1) % size) for i in range(size if wrap else size - 1)]
        down = [(j, i) for i, j in up]
        last = lax.slice_in_dim(array, length - width, length, axis=dim)
        leading = lax.slice_in_dim(array, 0, width, axis=dim)
        before = lax.ppermute(last, axis, up)
        after = lax.ppermute(leading, axis, down)
        array = jnp.concatenate([before, array, after], axis=dim)
    return array


def pad_cycle(stacked):
    wide = with_halo(stacked, (("lon", 3),), 1, True)
    return with_halo(wide, (("lat", 2),), 1, False)


def conv_taps(padded, kernel, flipped):
    band_rows = padded.shape[1] - 2
    band_cols = padded.shape[2] - 2
    total = jnp.zeros((padded.shape[0], band_rows, band_cols, kernel.shape[2]), F32)
    for row_off in range(3):
        for col_off in range(3):
            window = padded[:, row_off : row_off + band_rows, col_off : col_off + band_cols, :]
            tap = 3 * row_off + col_off
            total = total + jnp.einsum(
                "bijd,cd->bijc" if flipped else "bijc,cd->bijd",
                window,
                kernel[8 - tap if flipped else tap],
                preferred_element_type=F32,
            )
    return total


def kernel_terms(padded, grad_field):
    band_rows = grad_field.shape[1]
    band_cols = grad_field.shape[2]
    result = []
    for row_off in range(3):
        for col_off in range(3):
            window = padded[:, row_off : row_off + band_rows, col_off : col_off + band_cols, :]
            result.append(jnp.einsum("bijc,bijd->cd", window, grad_field, preferred_element_type=F32))
    return jnp.stack(result)


def general_body(state, upstream, first_kernel, second_kernel):
    scale_factor = 1.0 / math.sqrt(
        state.shape[1] * lax.axis_size("lat") * state.shape[2] * lax.axis_size("lon")
    )
    both_pad = pad_cycle(jnp.stack([state, upstream]))
    pre = conv_taps(both_pad[0], first_kernel, False)
    active = jax.nn.silu(pre).astype(BF16)
    back_act = conv_taps(both_pad[1], second_kernel, True)
    sigma = jax.nn.sigmoid(pre)
    back_pre = (back_act * sigma * (1.0 + pre * (1.0 - sigma))).astype(BF16)
    inner_pad = pad_cycle(jnp.stack([active, back_pre]))
    output_state = (state.astype(F32) + conv_taps(inner_pad[0], second_kernel, False)).astype(BF16)
    state_grad = (upstream.astype(F32) + conv_taps(inner_pad[1], first_kernel, True)).astype(BF16)
    summed = []
    for terms in (kernel_terms(both_pad[0], back_pre), kernel_terms(inner_pad[0], upstream)):
        part = lax.psum_scatter(terms, "lat", scatter_dimension=1, tiled=True)
        part = lax.psum_scatter(part, "lon", scatter_dimension=2, tiled=True)
        summed.append(part * scale_factor)
    return (output_state, state_grad, summed[0], summed[1])


def stage_plan(lat_size, chans, lon_first):
    bits = lat_size.bit_length() - 1
    order = [0, "lon", 1] if lon_first else [0, 1, "lon"]
    order += list(range(2, bits))
    plan, length, cols = [], lat_size, chans
    for op in order:
        plan.append((op, length, cols))
        if op == "lon":
            cols //= 2
        else:
            length //= 2
    return plan


PIECES = (((2, 0), (2, 2), (1, 1)), ((2, 1), (1, 0), (1, 2)))
ORDER = ((0, 0), (1, 0), (0, 1), (1, 1), (0, 2), (1, 2))


def fused_kernel(lat_size, scale, plans, names, *refs):
    r = dict(zip(names, refs))
    z = r["z"]
    batch, padded_rows, cols = z.shape[1], z.shape[2], z.shape[3]
    rows = padded_rows - 2
    chans = z.shape[4] // 3
    mid = slice(chans, 2 * chans)
    n_stage = 2 * padded_rows
    lat, lon = lax.axis_index("lat"), lax.axis_index("lon")
    other_lon = 1 - lon
    bits = lat_size.bit_length() - 1

    def bit_of(k):
        return lax.rem(lax.div(lat, 2**k), 2)

    def partner(k):
        return lat + (1 - 2 * bit_of(k)) * 2**k

    loads = [
        pltpu.make_async_copy(r["state"], z.at[0, :, 1 : rows + 1, :, mid], r["load_sem"].at[0]),
        pltpu.make_async_copy(r["upstream"], z.at[1, :, 1 : rows + 1, :, mid], r["load_sem"].at[1]),
        pltpu.make_async_copy(r["k1"], r["w1"], r["load_sem"].at[2]),
        pltpu.make_async_copy(r["k2"], r["w2"], r["load_sem"].at[3]),
    ]
    for load in loads:
        load.start()

    barrier = pltpu.get_barrier_semaphore()

    def greet(to_lat, to_lon):
        pl.semaphore_signal(barrier, inc=1, device_id=(to_lat, to_lon), device_id_type=MESH)

    greet(lat, other_lon)
    for k in range(1, bits):
        greet(partner(k), lon)

    @pl.when(lat > 0)
    def _():
        greet(lat - 1, lon)
        greet(lat - 1, other_lon)

    @pl.when(lat < lat_size - 1)
    def _():
        greet(lat + 1, lon)
        greet(lat + 1, other_lon)

    beside = jnp.where(lat > 0, 2, 0) + jnp.where(lat < lat_size - 1, 2, 0)
    pl.semaphore_wait(barrier, bits + beside)

    def row_copy(pair, f, up):
        src, dst = (rows, 0) if up else (1, rows + 1)
        return pltpu.make_async_remote_copy(
            src_ref=z.at[2 * pair + f, :, src, :, mid],
            dst_ref=z.at[2 * pair + f, :, dst, :, mid],
            send_sem=r["row_send"].at[pair, f, int(up)],
            recv_sem=r["row_recv"].at[pair, f, int(up)],
            device_id=(lat + 1 if up else lat - 1, lon),
            device_id_type=MESH,
        )

    def rim_copy(pair):
        return pltpu.make_async_remote_copy(
            src_ref=r["rim_out"].at[pair],
            dst_ref=r["rim_in"].at[pair],
            send_sem=r["rim_send"].at[pair],
            recv_sem=r["rim_recv"].at[pair],
            device_id=(lat, other_lon),
            device_id_type=MESH,
        )

    def corner_copy(pair, up):
        return pltpu.make_async_remote_copy(
            src_ref=r["corner_out"].at[pair, int(up)],
            dst_ref=r["corner_in"].at[pair, int(up)],
            send_sem=r["corner_send"].at[pair, int(up)],
            recv_sem=r["corner_recv"].at[pair, int(up)],
            device_id=(lat + 1 if up else lat - 1, other_lon),
            device_id_type=MESH,
        )

    def both_ways(up_copies, down_copies, what, mirrored):
        @pl.when(lat < lat_size - 1)
        def _():
            for c in down_copies if mirrored else up_copies:
                getattr(c, what)()

        @pl.when(lat > 0)
        def _():
            for c in up_copies if mirrored else down_copies:
                getattr(c, what)()

    def copies(pair):
        ups = [corner_copy(pair, True)] + [row_copy(pair, f, True) for f in range(2)]
        downs = [corner_copy(pair, False)] + [row_copy(pair, f, False) for f in range(2)]
        return ups, downs, [rim_copy(pair)]

    def send_halo(pair):
        for f in range(2):
            for side, lo, pick in ((1, 0, 0), (0, cols - 16, 15)):
                for b in range(batch):
                    for i in range(1, rows + 1):
                        block = z[2 * pair + f, b, i, lo : lo + 16, mid].astype(F32)
                        r["rim32"][f, side, 2 * i + b : 2 * i + b + 1, :] = block[pick : pick + 1]
        for f in range(2):
            for side in range(2):
                r["rim_out"][pair, side, f] = r["rim32"][f, side].astype(BF16)
                k = 2 * (2 * side + f)
                r["corner32"][0, k : k + 2] = r["rim32"][f, side, 2:4]
                r["corner32"][1, k : k + 2] = r["rim32"][f, side, n_stage - 4 : n_stage - 2]
        for up in range(2):
            r["corner_out"][pair, up] = r["corner32"][up].astype(BF16)
        ups, downs, flats = copies(pair)
        for c in flats:
            c.start()
        both_ways(ups, downs, "start", False)

    def shift_rows(pair, row_list):
        for f in range(2):
            fld = 2 * pair + f
            for b in range(batch):
                for i in row_list:
                    x = z[fld, b, i, :, mid].astype(F32)
                    z[fld, b, i, :, 0:chans] = pltpu.roll(x, 1, 0).astype(BF16)
                    z[fld, b, i, :, 2 * chans :] = pltpu.roll(x, cols - 1, 0).astype(BF16)

    def receive_halo(pair):
        ups, downs, flats = copies(pair)
        for c in flats:
            c.wait_recv()
        both_ways(ups, downs, "wait_recv", True)
        zero_row = jnp.zeros((batch, cols, chans), BF16)

        @pl.when(lat == 0)
        def _():
            r["corner_in"][pair, 1] = jnp.zeros((16, chans), BF16)
            for f in range(2):
                z[2 * pair + f, :, 0, :, mid] = zero_row

        @pl.when(lat == lat_size - 1)
        def _():
            r["corner_in"][pair, 0] = jnp.zeros((16, chans), BF16)
            for f in range(2):
                z[2 * pair + f, :, rows + 1, :, mid] = zero_row

        for up in range(2):
            r["corner32"][up] = r["corner_in"][pair, up].astype(F32)
        for f in range(2):
            for s in range(2):
                k = 2 * (2 * s + f)
                r["rim32"][f, s] = r["rim_in"][pair, s, f].astype(F32)
                r["rim32"][f, s, 0:2] = r["corner32"][1, k : k + 2]
                r["rim32"][f, s, n_stage - 2 :] = r["corner32"][0, k : k + 2]
        shift_rows(pair, (0, rows + 1))
        first = lax.broadcasted_iota(jnp.int32, (16, chans), 0) == 0
        final = lax.broadcasted_iota(jnp.int32, (16, chans), 0) == 15
        for f in range(2):
            fld = 2 * pair + f
            for b in range(batch):
                for i in range(padded_rows):
                    k = 2 * i + b
                    old = z[fld, b, i, 0:16, 0:chans].astype(F32)
                    z[fld, b, i, 0:16, 0:chans] = jnp.where(first, r["rim32"][f, 0, k : k + 1], old).astype(BF16)
                    old = z[fld, b, i, cols - 16 :, 2 * chans :].astype(F32)
                    z[fld, b, i, cols - 16 :, 2 * chans :] = jnp.where(
                        final, r["rim32"][f, 1, k : k + 1], old
                    ).astype(BF16)

    def finish_halo(pair):
        ups, downs, flats = copies(pair)
        for c in flats:
            c.wait_send()
        both_ways(ups, downs, "wait_send", False)

    def stage_copy(grp, s, p):
        op = plans[grp][s][0]
        to = (lat, other_lon) if op == "lon" else (partner(op), lon)
        return pltpu.make_async_remote_copy(
            src_ref=r[f"send{grp}{s}"].at[p],
            dst_ref=r[f"recv{grp}{s}"].at[p],
            send_sem=r["rs_send"].at[grp, s, p],
            recv_sem=r["rs_recv"].at[grp, s, p],
            device_id=to,
            device_id_type=MESH,
        )

    def half(grp, s, p, mine):
        op, length, width = plans[grp][s]
        keep = r[f"keep{grp}{s}"]
        if op == "lon":
            start = pl.multiple_of((lon if mine else other_lon) * (width // 2), width // 2)
            return keep[p, :, :, :, pl.ds(start, width // 2)]
        which = bit_of(op) if mine else 1 - bit_of(op)
        return keep[p, :, :, which]

    def put(grp, s, p, value):
        keep = r[f"keep{grp}{s}"]
        keep[p] = value.reshape(keep.shape[1:])
        r[f"send{grp}{s}"][p] = half(grp, s, p, False).astype(BF16)
        stage_copy(grp, s, p).start()

    def advance(grp, s, p):
        stage_copy(grp, s, p).wait_recv()
        value = half(grp, s, p, True) + r[f"recv{grp}{s}"][p].astype(F32)
        if s + 1 < len(plans[grp]):
            put(grp, s + 1, p, value)
            return
        value = (value * scale).reshape(3, value.shape[2], value.shape[3])
        grad, e = PIECES[grp][p]
        if grad == 2:
            for f in range(3):
                r["g2"][8 - 3 * e - f] = value[f]
        else:
            r["g1"][3 * e : 3 * e + 3] = value

    def window(fld, e):
        return z[fld, :, e : e + rows].reshape(batch * rows * cols, 3 * chans)

    def conv(fld, w, b):
        total = None
        for e in range(3):
            x = z[fld, b, e : e + rows].reshape(rows * cols, 3 * chans)
            part = jnp.dot(x, w[3 * e : 3 * e + 3].reshape(3 * chans, chans), preferred_element_type=F32)
            total = part if total is None else total + part
        return total

    loads[0].wait()
    loads[1].wait()
    send_halo(0)
    shift_rows(0, range(1, rows + 1))
    loads[2].wait()
    loads[3].wait()
    for t in range(9):
        r["w1t"][8 - t] = r["w1"][t].T
        r["w2t"][8 - t] = r["w2"][t].T
    receive_halo(0)

    for b in range(batch):
        pre = conv(0, r["w1"], b)
        sigma = 1.0 / (1.0 + jnp.exp(-pre))
        active = (pre * sigma).astype(BF16)
        z[2, b, 1 : rows + 1, :, mid] = active.reshape(rows, cols, chans)
        r["slope"][b] = sigma * (1.0 + pre * (1.0 - sigma))
    act = z[2, :, 1 : rows + 1, :, mid].reshape(batch * rows * cols, chans)
    for e in range(3):
        terms = lax.dot_general(act, window(1, e), (((0,), (0,)), ((), ())), preferred_element_type=F32)
        grp, p = ORDER[e]
        put(grp, 0, p, jnp.stack([terms[:, f * chans : (f + 1) * chans] for f in range(3)]))
    for b in range(batch):
        back = (conv(1, r["w2t"], b) * r["slope"][b]).astype(BF16)
        z[3, b, 1 : rows + 1, :, mid] = back.reshape(rows, cols, chans)
    send_halo(1)

    def advance_all(s, pieces):
        for grp, p in pieces:
            advance(grp, s, p)

    early, late = ORDER[:3], ORDER[3:]
    advance_all(0, early)
    back = z[3, :, 1 : rows + 1, :, mid].reshape(batch * rows * cols, chans)
    for e in range(3):
        terms = lax.dot_general(window(0, e), back, (((0,), (0,)), ((), ())), preferred_element_type=F32)
        grp, p = late[e]
        put(grp, 0, p, terms)
    advance_all(0, late)
    advance_all(1, early)
    shift_rows(1, range(1, rows + 1))
    receive_halo(1)

    def finish_field(fld, w, name, b):
        near = z[fld, b, 1 : rows + 1, :, mid].astype(F32)
        r[name][b] = (near + conv(fld + 2, w, b).reshape(rows, cols, chans)).astype(BF16)

    finish_field(0, r["w2"], "out", 0)
    advance_all(1, late)
    finish_field(0, r["w2"], "out", 1)
    advance_all(2, early)
    finish_field(1, r["w1t"], "sgrad", 0)
    advance_all(2, late)
    finish_field(1, r["w1t"], "sgrad", 1)
    for s in range(3, len(plans[0])):
        advance_all(s, early)
        advance_all(s, late)
    for pair in range(2):
        finish_halo(pair)
    for grp in range(2):
        for s in range(len(plans[grp])):
            for e in range(3):
                stage_copy(grp, s, e).wait_send()


def fused_body(state, upstream, first_kernel, second_kernel):
    lat_size, lon_size = lax.axis_size("lat"), lax.axis_size("lon")
    batch, rows, cols, chans = state.shape
    scale = 1.0 / math.sqrt(rows * lat_size * cols * lon_size)
    own = chans // lat_size
    n_stage = 2 * (rows + 2)
    plans = [stage_plan(lat_size, chans, True), stage_plan(lat_size, chans, False)]
    steps = len(plans[0])
    scratch = {
        "z": pltpu.VMEM((4, batch, rows + 2, cols, 3 * chans), BF16),
        "w1": pltpu.VMEM((9, chans, chans), BF16),
        "w2": pltpu.VMEM((9, chans, chans), BF16),
        "w1t": pltpu.VMEM((9, chans, chans), BF16),
        "w2t": pltpu.VMEM((9, chans, chans), BF16),
        "slope": pltpu.VMEM((batch, rows * cols, chans), F32),
        "rim32": pltpu.VMEM((2, 2, n_stage, chans), F32),
        "rim_out": pltpu.VMEM((2, 2, 2, n_stage, chans), BF16),
        "rim_in": pltpu.VMEM((2, 2, 2, n_stage, chans), BF16),
        "corner32": pltpu.VMEM((2, 16, chans), F32),
        "corner_out": pltpu.VMEM((2, 2, 16, chans), BF16),
        "corner_in": pltpu.VMEM((2, 2, 16, chans), BF16),
        "load_sem": pltpu.SemaphoreType.DMA((4,)),
        "row_send": pltpu.SemaphoreType.DMA((2, 2, 2)),
        "row_recv": pltpu.SemaphoreType.DMA((2, 2, 2)),
        "rim_send": pltpu.SemaphoreType.DMA((2,)),
        "rim_recv": pltpu.SemaphoreType.DMA((2,)),
        "corner_send": pltpu.SemaphoreType.DMA((2, 2)),
        "corner_recv": pltpu.SemaphoreType.DMA((2, 2)),
        "rs_send": pltpu.SemaphoreType.DMA((2, steps, 3)),
        "rs_recv": pltpu.SemaphoreType.DMA((2, steps, 3)),
    }
    for grp in range(2):
        for s, (op, length, width) in enumerate(plans[grp]):
            if op == "lon":
                kept, sent = (3, length, own, width), (3, length, own, width // 2)
            else:
                kept, sent = (3, length // 2, 2, own, width), (3, length // 2, own, width)
            scratch[f"keep{grp}{s}"] = pltpu.VMEM((3,) + kept, F32)
            scratch[f"send{grp}{s}"] = pltpu.VMEM((3,) + sent, BF16)
            scratch[f"recv{grp}{s}"] = pltpu.VMEM((3,) + sent, BF16)
    names = ["state", "upstream", "k1", "k2", "out", "sgrad", "g1", "g2"] + list(scratch)

    def kernel(*refs):
        fused_kernel(lat_size, scale, plans, names, *refs)

    vmem = pl.BlockSpec(memory_space=pltpu.VMEM)
    anywhere = pl.BlockSpec(memory_space=pltpu.HBM)
    kinds = [(state.shape, BF16)] * 2 + [((9, own, chans // 2), F32)] * 2
    held = pl.pallas_call(
        kernel,
        out_shape=tuple(pltpu.VMEM(shape, kind) for shape, kind in kinds),
        in_specs=[anywhere] * 4,
        out_specs=(vmem,) * 4,
        scratch_shapes=list(scratch.values()),
        compiler_params=pltpu.CompilerParams(
            collective_id=0, has_side_effects=True, vmem_limit_bytes=52 * 2**20
        ),
    )(state, upstream, first_kernel, second_kernel)

    def write_out(*refs):
        moves = [pltpu.make_async_copy(refs[i], refs[4 + i], refs[8].at[i]) for i in range(4)]
        for move in moves:
            move.start()
        for move in moves:
            move.wait()

    return pl.pallas_call(
        write_out,
        out_shape=tuple(jax.ShapeDtypeStruct(shape, kind) for shape, kind in kinds),
        in_specs=[vmem] * 4,
        out_specs=(anywhere,) * 4,
        scratch_shapes=[pltpu.SemaphoreType.DMA((4,))],
    )(*[pltpu.with_memory_space_constraint(h, pltpu.VMEM) for h in held])


def body(state, upstream, first_kernel, second_kernel):
    lat_size, lon_size = lax.axis_size("lat"), lax.axis_size("lon")
    batch, rows, cols, chans = state.shape
    fits = (
        lon_size == 2
        and lat_size >= 4
        and lat_size & (lat_size - 1) == 0
        and batch == 2
        and 2 * (rows + 2) == 16
        and cols % 16 == 0
        and chans % (16 * lat_size) == 0
        and (chans // 2) % 128 == 0
    )
    run = fused_body if fits else general_body
    return run(state, upstream, first_kernel, second_kernel)


def solution(mesh):
    placed = (P(None, "lat", "lon", None), P(None, "lat", "lon", None), P(), P())
    return jax.shard_map(
        body,
        mesh=mesh,
        in_specs=placed,
        out_specs=(
            P(None, "lat", "lon", None),
            P(None, "lat", "lon", None),
            P(None, "lat", "lon"),
            P(None, "lat", "lon"),
        ),
        check_vma=False,
    )
```

```python
import math

import jax
import jax.numpy as jnp
from jax import lax
from jax.experimental import pallas as pl
from jax.experimental.pallas import tpu as pltpu
from jax.sharding import PartitionSpec as P

F32 = jnp.float32
BF16 = jnp.bfloat16
MESH = pl.DeviceIdType.MESH


def with_halo(array, sides, width, wrap):
    for axis, dim in sides:
        size, length = (lax.axis_size(axis), array.shape[dim])
        up = [(i, (i + 1) % size) for i in range(size if wrap else size - 1)]
        down = [(j, i) for i, j in up]
        last = lax.slice_in_dim(array, length - width, length, axis=dim)
        leading = lax.slice_in_dim(array, 0, width, axis=dim)
        before = lax.ppermute(last, axis, up)
        after = lax.ppermute(leading, axis, down)
        array = jnp.concatenate([before, array, after], axis=dim)
    return array


def pad_cycle(stacked):
    wide = with_halo(stacked, (("lon", 3),), 1, True)
    return with_halo(wide, (("lat", 2),), 1, False)


def conv_taps(padded, kernel, flipped):
    band_rows = padded.shape[1] - 2
    band_cols = padded.shape[2] - 2
    total = jnp.zeros((padded.shape[0], band_rows, band_cols, kernel.shape[2]), F32)
    for row_off in range(3):
        for col_off in range(3):
            window = padded[:, row_off : row_off + band_rows, col_off : col_off + band_cols, :]
            tap = 3 * row_off + col_off
            total = total + jnp.einsum(
                "bijd,cd->bijc" if flipped else "bijc,cd->bijd",
                window,
                kernel[8 - tap if flipped else tap],
                preferred_element_type=F32,
            )
    return total


def kernel_terms(padded, grad_field):
    band_rows = grad_field.shape[1]
    band_cols = grad_field.shape[2]
    result = []
    for row_off in range(3):
        for col_off in range(3):
            window = padded[:, row_off : row_off + band_rows, col_off : col_off + band_cols, :]
            result.append(jnp.einsum("bijc,bijd->cd", window, grad_field, preferred_element_type=F32))
    return jnp.stack(result)


def general_body(state, upstream, first_kernel, second_kernel):
    scale_factor = 1.0 / math.sqrt(
        state.shape[1] * lax.axis_size("lat") * state.shape[2] * lax.axis_size("lon")
    )
    both_pad = pad_cycle(jnp.stack([state, upstream]))
    pre = conv_taps(both_pad[0], first_kernel, False)
    active = jax.nn.silu(pre).astype(BF16)
    back_act = conv_taps(both_pad[1], second_kernel, True)
    sigma = jax.nn.sigmoid(pre)
    back_pre = (back_act * sigma * (1.0 + pre * (1.0 - sigma))).astype(BF16)
    inner_pad = pad_cycle(jnp.stack([active, back_pre]))
    output_state = (state.astype(F32) + conv_taps(inner_pad[0], second_kernel, False)).astype(BF16)
    state_grad = (upstream.astype(F32) + conv_taps(inner_pad[1], first_kernel, True)).astype(BF16)
    summed = []
    for terms in (kernel_terms(both_pad[0], back_pre), kernel_terms(inner_pad[0], upstream)):
        part = lax.psum_scatter(terms, "lat", scatter_dimension=1, tiled=True)
        part = lax.psum_scatter(part, "lon", scatter_dimension=2, tiled=True)
        summed.append(part * scale_factor)
    return (output_state, state_grad, summed[0], summed[1])


def stage_plan(lat_size, chans, first):
    bits = lat_size.bit_length() - 1
    turns = [["lon"], [1], list(range(2, bits))]
    order = [0]
    for turn in (turns, turns[1:] + turns[:1], turns[2:] + turns[:2])[first]:
        order += turn
    left, plan, cols = list(range(bits)), [], chans
    for op in order:
        if op == "lon":
            plan.append((op, 2 ** len(left), 1, cols))
            cols //= 2
        else:
            at = left.index(op)
            plan.append((op, 2 ** (len(left) - 1 - at), 2**at, cols))
            left.remove(op)
    return plan


PIECES = (((2, 0), (1, 0)), ((2, 1), (1, 1)), ((2, 2), (1, 2)))
ORDER = ((0, 0), (1, 0), (2, 0), (0, 1), (1, 1), (2, 1))


def fused_kernel(lat_size, scale, plans, names, *refs):
    r = dict(zip(names, refs))
    z = r["z"]
    batch, padded_rows, cols = z.shape[1], z.shape[2], z.shape[3]
    rows = padded_rows - 2
    chans = z.shape[4] // 3
    mid = slice(chans, 2 * chans)
    n_stage = 2 * padded_rows
    lat, lon = lax.axis_index("lat"), lax.axis_index("lon")
    other_lon = 1 - lon
    bits = lat_size.bit_length() - 1

    def bit_of(k):
        return lax.rem(lax.div(lat, 2**k), 2)

    def partner(k):
        return lat + (1 - 2 * bit_of(k)) * 2**k

    loads = [
        pltpu.make_async_copy(r["state"], z.at[0, :, 1 : rows + 1, :, mid], r["load_sem"].at[0]),
        pltpu.make_async_copy(r["upstream"], z.at[1, :, 1 : rows + 1, :, mid], r["load_sem"].at[1]),
        pltpu.make_async_copy(r["k1"], r["w1"], r["load_sem"].at[2]),
        pltpu.make_async_copy(r["k2"], r["w2"], r["load_sem"].at[3]),
    ]
    for load in loads:
        load.start()

    barrier = pltpu.get_barrier_semaphore()

    def greet(to_lat, to_lon):
        pl.semaphore_signal(barrier, inc=1, device_id=(to_lat, to_lon), device_id_type=MESH)

    greet(lat, other_lon)
    for k in range(1, bits):
        greet(partner(k), lon)

    @pl.when(lat > 0)
    def _():
        greet(lat - 1, lon)
        greet(lat - 1, other_lon)

    @pl.when(lat < lat_size - 1)
    def _():
        greet(lat + 1, lon)
        greet(lat + 1, other_lon)

    beside = jnp.where(lat > 0, 2, 0) + jnp.where(lat < lat_size - 1, 2, 0)
    pl.semaphore_wait(barrier, bits + beside)

    def row_copy(pair, f, up):
        src, dst = (rows, 0) if up else (1, rows + 1)
        return pltpu.make_async_remote_copy(
            src_ref=z.at[2 * pair + f, :, src, :, mid],
            dst_ref=z.at[2 * pair + f, :, dst, :, mid],
            send_sem=r["row_send"].at[pair, f, int(up)],
            recv_sem=r["row_recv"].at[pair, f, int(up)],
            device_id=(lat + 1 if up else lat - 1, lon),
            device_id_type=MESH,
        )

    def rim_copy(pair):
        return pltpu.make_async_remote_copy(
            src_ref=r["rim_out"].at[pair],
            dst_ref=r["rim_in"].at[pair],
            send_sem=r["rim_send"].at[pair],
            recv_sem=r["rim_recv"].at[pair],
            device_id=(lat, other_lon),
            device_id_type=MESH,
        )

    def corner_copy(pair, up):
        return pltpu.make_async_remote_copy(
            src_ref=r["corner_out"].at[pair, int(up)],
            dst_ref=r["corner_in"].at[pair, int(up)],
            send_sem=r["corner_send"].at[pair, int(up)],
            recv_sem=r["corner_recv"].at[pair, int(up)],
            device_id=(lat + 1 if up else lat - 1, other_lon),
            device_id_type=MESH,
        )

    def both_ways(up_copies, down_copies, what, mirrored):
        @pl.when(lat < lat_size - 1)
        def _():
            for c in down_copies if mirrored else up_copies:
                getattr(c, what)()

        @pl.when(lat > 0)
        def _():
            for c in up_copies if mirrored else down_copies:
                getattr(c, what)()

    def copies(pair):
        ups = [corner_copy(pair, True)] + [row_copy(pair, f, True) for f in range(2)]
        downs = [corner_copy(pair, False)] + [row_copy(pair, f, False) for f in range(2)]
        return ups, downs, [rim_copy(pair)]

    def send_halo(pair):
        for f in range(2):
            for side, lo, pick in ((1, 0, 0), (0, cols - 16, 15)):
                for b in range(batch):
                    for i in range(1, rows + 1):
                        block = z[2 * pair + f, b, i, lo : lo + 16, mid].astype(F32)
                        r["rim32"][f, side, 2 * i + b : 2 * i + b + 1, :] = block[pick : pick + 1]
        for f in range(2):
            for side in range(2):
                r["rim_out"][pair, side, f] = r["rim32"][f, side].astype(BF16)
                k = 2 * (2 * side + f)
                r["corner32"][0, k : k + 2] = r["rim32"][f, side, 2:4]
                r["corner32"][1, k : k + 2] = r["rim32"][f, side, n_stage - 4 : n_stage - 2]
        for up in range(2):
            r["corner_out"][pair, up] = r["corner32"][up].astype(BF16)
        ups, downs, flats = copies(pair)
        for c in flats:
            c.start()
        both_ways(ups, downs, "start", False)

    def shift_rows(pair, row_list):
        for f in range(2):
            fld = 2 * pair + f
            for b in range(batch):
                for i in row_list:
                    x = z[fld, b, i, :, mid].astype(F32)
                    z[fld, b, i, :, 0:chans] = pltpu.roll(x, 1, 0).astype(BF16)
                    z[fld, b, i, :, 2 * chans :] = pltpu.roll(x, cols - 1, 0).astype(BF16)

    def receive_halo(pair):
        ups, downs, flats = copies(pair)
        for c in flats:
            c.wait_recv()
        both_ways(ups, downs, "wait_recv", True)
        zero_row = jnp.zeros((batch, cols, chans), BF16)

        @pl.when(lat == 0)
        def _():
            r["corner_in"][pair, 1] = jnp.zeros((16, chans), BF16)
            for f in range(2):
                z[2 * pair + f, :, 0, :, mid] = zero_row

        @pl.when(lat == lat_size - 1)
        def _():
            r["corner_in"][pair, 0] = jnp.zeros((16, chans), BF16)
            for f in range(2):
                z[2 * pair + f, :, rows + 1, :, mid] = zero_row

        for up in range(2):
            r["corner32"][up] = r["corner_in"][pair, up].astype(F32)
        for f in range(2):
            for s in range(2):
                k = 2 * (2 * s + f)
                r["rim32"][f, s] = r["rim_in"][pair, s, f].astype(F32)
                r["rim32"][f, s, 0:2] = r["corner32"][1, k : k + 2]
                r["rim32"][f, s, n_stage - 2 :] = r["corner32"][0, k : k + 2]
        shift_rows(pair, (0, rows + 1))
        first = lax.broadcasted_iota(jnp.int32, (16, chans), 0) == 0
        final = lax.broadcasted_iota(jnp.int32, (16, chans), 0) == 15
        for f in range(2):
            fld = 2 * pair + f
            for b in range(batch):
                for i in range(padded_rows):
                    k = 2 * i + b
                    old = z[fld, b, i, 0:16, 0:chans].astype(F32)
                    z[fld, b, i, 0:16, 0:chans] = jnp.where(first, r["rim32"][f, 0, k : k + 1], old).astype(BF16)
                    old = z[fld, b, i, cols - 16 :, 2 * chans :].astype(F32)
                    z[fld, b, i, cols - 16 :, 2 * chans :] = jnp.where(
                        final, r["rim32"][f, 1, k : k + 1], old
                    ).astype(BF16)

    def finish_halo(pair):
        ups, downs, flats = copies(pair)
        for c in flats:
            c.wait_send()
        both_ways(ups, downs, "wait_send", False)

    def stage_copy(grp, s, p):
        op = plans[grp][s][0]
        to = (lat, other_lon) if op == "lon" else (partner(op), lon)
        return pltpu.make_async_remote_copy(
            src_ref=r[f"send{grp}{s}"].at[p],
            dst_ref=r[f"recv{grp}{s}"].at[p],
            send_sem=r["rs_send"].at[grp, s, p],
            recv_sem=r["rs_recv"].at[grp, s, p],
            device_id=to,
            device_id_type=MESH,
        )

    def half(grp, s, p, mine):
        op, _, _, width = plans[grp][s]
        keep = r[f"keep{grp}{s}"]
        if op == "lon":
            start = pl.multiple_of((lon if mine else other_lon) * (width // 2), width // 2)
            return keep[p, :, :, :, :, pl.ds(start, width // 2)]
        which = bit_of(op) if mine else 1 - bit_of(op)
        return keep[p, :, :, which]

    def put(grp, s, p, value):
        keep = r[f"keep{grp}{s}"]
        keep[p] = value.reshape(keep.shape[1:])
        r[f"send{grp}{s}"][p] = half(grp, s, p, False).astype(BF16)
        stage_copy(grp, s, p).start()

    def advance(grp, s, p):
        stage_copy(grp, s, p).wait_recv()
        value = half(grp, s, p, True) + r[f"recv{grp}{s}"][p].astype(F32)
        if s + 1 < len(plans[grp]):
            put(grp, s + 1, p, value)
            return
        value = (value * scale).reshape(3, value.shape[-2], value.shape[-1])
        grad, e = PIECES[grp][p]
        if grad == 2:
            for f in range(3):
                r["g2"][8 - 3 * e - f] = value[f]
        else:
            r["g1"][3 * e : 3 * e + 3] = value

    def window(fld, e):
        return z[fld, :, e : e + rows].reshape(batch * rows * cols, 3 * chans)

    def conv(fld, w, b):
        total = None
        for e in range(3):
            x = z[fld, b, e : e + rows].reshape(rows * cols, 3 * chans)
            part = jnp.dot(x, w[3 * e : 3 * e + 3].reshape(3 * chans, chans), preferred_element_type=F32)
            total = part if total is None else total + part
        return total

    loads[0].wait()
    loads[1].wait()
    send_halo(0)
    shift_rows(0, range(1, rows + 1))
    loads[2].wait()
    loads[3].wait()
    for t in range(9):
        r["w1t"][8 - t] = r["w1"][t].T
        r["w2t"][8 - t] = r["w2"][t].T
    receive_halo(0)

    for b in range(batch):
        pre = conv(0, r["w1"], b)
        sigma = 1.0 / (1.0 + jnp.exp(-pre))
        active = (pre * sigma).astype(BF16)
        z[2, b, 1 : rows + 1, :, mid] = active.reshape(rows, cols, chans)
        r["slope"][b] = sigma * (1.0 + pre * (1.0 - sigma))
    act = z[2, :, 1 : rows + 1, :, mid].reshape(batch * rows * cols, chans)
    for e in range(3):
        terms = lax.dot_general(act, window(1, e), (((0,), (0,)), ((), ())), preferred_element_type=F32)
        grp, p = ORDER[e]
        put(grp, 0, p, jnp.stack([terms[:, f * chans : (f + 1) * chans] for f in range(3)]))
    early, late = ORDER[:3], ORDER[3:]

    def advance_all(s, pieces):
        for grp, p in pieces:
            advance(grp, s, p)

    for b in range(batch):
        back = (conv(1, r["w2t"], b) * r["slope"][b]).astype(BF16)
        z[3, b, 1 : rows + 1, :, mid] = back.reshape(rows, cols, chans)
        if b == 0:
            advance_all(0, early)
    back = z[3, :, 1 : rows + 1, :, mid].reshape(batch * rows * cols, chans)
    for e in range(3):
        terms = lax.dot_general(window(0, e), back, (((0,), (0,)), ((), ())), preferred_element_type=F32)
        grp, p = late[e]
        put(grp, 0, p, terms)
    send_halo(1)
    advance_all(0, late)
    advance_all(1, early)
    shift_rows(1, range(1, rows + 1))
    advance_all(1, late)
    receive_halo(1)
    advance_all(2, early)

    def finish_field(fld, w, name, b):
        near = z[fld, b, 1 : rows + 1, :, mid].astype(F32)
        r[name][b] = (near + conv(fld + 2, w, b).reshape(rows, cols, chans)).astype(BF16)

    finish_field(0, r["w2"], "out", 0)
    advance_all(2, late)
    finish_field(0, r["w2"], "out", 1)
    advance_all(3, early)
    finish_field(1, r["w1t"], "sgrad", 0)
    advance_all(3, late)
    finish_field(1, r["w1t"], "sgrad", 1)
    for s in range(4, len(plans[0])):
        advance_all(s, early)
        advance_all(s, late)
    for pair in range(2):
        finish_halo(pair)
    for grp in range(3):
        for s in range(len(plans[grp])):
            for p in range(2):
                stage_copy(grp, s, p).wait_send()


def fused_body(state, upstream, first_kernel, second_kernel):
    lat_size, lon_size = lax.axis_size("lat"), lax.axis_size("lon")
    batch, rows, cols, chans = state.shape
    scale = 1.0 / math.sqrt(rows * lat_size * cols * lon_size)
    own = chans // lat_size
    n_stage = 2 * (rows + 2)
    plans = [stage_plan(lat_size, chans, first) for first in range(3)]
    steps = len(plans[0])
    scratch = {
        "z": pltpu.VMEM((4, batch, rows + 2, cols, 3 * chans), BF16),
        "w1": pltpu.VMEM((9, chans, chans), BF16),
        "w2": pltpu.VMEM((9, chans, chans), BF16),
        "w1t": pltpu.VMEM((9, chans, chans), BF16),
        "w2t": pltpu.VMEM((9, chans, chans), BF16),
        "slope": pltpu.VMEM((batch, rows * cols, chans), F32),
        "rim32": pltpu.VMEM((2, 2, n_stage, chans), F32),
        "rim_out": pltpu.VMEM((2, 2, 2, n_stage, chans), BF16),
        "rim_in": pltpu.VMEM((2, 2, 2, n_stage, chans), BF16),
        "corner32": pltpu.VMEM((2, 16, chans), F32),
        "corner_out": pltpu.VMEM((2, 2, 16, chans), BF16),
        "corner_in": pltpu.VMEM((2, 2, 16, chans), BF16),
        "load_sem": pltpu.SemaphoreType.DMA((4,)),
        "row_send": pltpu.SemaphoreType.DMA((2, 2, 2)),
        "row_recv": pltpu.SemaphoreType.DMA((2, 2, 2)),
        "rim_send": pltpu.SemaphoreType.DMA((2,)),
        "rim_recv": pltpu.SemaphoreType.DMA((2,)),
        "corner_send": pltpu.SemaphoreType.DMA((2, 2)),
        "corner_recv": pltpu.SemaphoreType.DMA((2, 2)),
        "rs_send": pltpu.SemaphoreType.DMA((3, steps, 2)),
        "rs_recv": pltpu.SemaphoreType.DMA((3, steps, 2)),
    }
    for grp in range(3):
        for s, (op, high, low, width) in enumerate(plans[grp]):
            if op == "lon":
                kept, sent = (2, 3, high, low, own, width), (2, 3, high, low, own, width // 2)
            else:
                kept, sent = (2, 3, high, 2, low, own, width), (2, 3, high, low, own, width)
            scratch[f"keep{grp}{s}"] = pltpu.VMEM(kept, F32)
            scratch[f"send{grp}{s}"] = pltpu.VMEM(sent, BF16)
            scratch[f"recv{grp}{s}"] = pltpu.VMEM(sent, BF16)
    names = ["state", "upstream", "k1", "k2", "out", "sgrad", "g1", "g2"] + list(scratch)

    def kernel(*refs):
        fused_kernel(lat_size, scale, plans, names, *refs)

    vmem = pl.BlockSpec(memory_space=pltpu.VMEM)
    anywhere = pl.BlockSpec(memory_space=pltpu.HBM)
    kinds = [(state.shape, BF16)] * 2 + [((9, own, chans // 2), F32)] * 2
    held = pl.pallas_call(
        kernel,
        out_shape=tuple(pltpu.VMEM(shape, kind) for shape, kind in kinds),
        in_specs=[anywhere] * 4,
        out_specs=(vmem,) * 4,
        scratch_shapes=list(scratch.values()),
        compiler_params=pltpu.CompilerParams(
            collective_id=0, has_side_effects=True, vmem_limit_bytes=56 * 2**20
        ),
    )(*[pltpu.with_memory_space_constraint(x, pltpu.HBM) for x in (state, upstream, first_kernel, second_kernel)])

    def write_out(*refs):
        moves = [pltpu.make_async_copy(refs[i], refs[4 + i], refs[8].at[i]) for i in range(4)]
        for move in moves:
            move.start()
        for move in moves:
            move.wait()

    return pl.pallas_call(
        write_out,
        out_shape=tuple(jax.ShapeDtypeStruct(shape, kind) for shape, kind in kinds),
        in_specs=[vmem] * 4,
        out_specs=(anywhere,) * 4,
        scratch_shapes=[pltpu.SemaphoreType.DMA((4,))],
    )(*[pltpu.with_memory_space_constraint(h, pltpu.VMEM) for h in held])


def body(state, upstream, first_kernel, second_kernel):
    lat_size, lon_size = lax.axis_size("lat"), lax.axis_size("lon")
    batch, rows, cols, chans = state.shape
    fits = (
        lon_size == 2
        and lat_size >= 16
        and lat_size & (lat_size - 1) == 0
        and batch == 2
        and 2 * (rows + 2) == 16
        and cols % 16 == 0
        and chans % (16 * lat_size) == 0
        and (chans // 2) % 128 == 0
    )
    run = fused_body if fits else general_body
    return run(state, upstream, first_kernel, second_kernel)


def solution(mesh):
    placed = (P(None, "lat", "lon", None), P(None, "lat", "lon", None), P(), P())
    return jax.shard_map(
        body,
        mesh=mesh,
        in_specs=placed,
        out_specs=(
            P(None, "lat", "lon", None),
            P(None, "lat", "lon", None),
            P(None, "lat", "lon"),
            P(None, "lat", "lon"),
        ),
        check_vma=False,
    )
```

```python
import math

import jax
import jax.numpy as jnp
from jax import lax
from jax.experimental import pallas as pl
from jax.experimental.pallas import tpu as pltpu
from jax.sharding import PartitionSpec as P

F32 = jnp.float32
BF16 = jnp.bfloat16
MESH = pl.DeviceIdType.MESH


def with_halo(array, sides, width, wrap):
    for axis, dim in sides:
        size, length = (lax.axis_size(axis), array.shape[dim])
        up = [(i, (i + 1) % size) for i in range(size if wrap else size - 1)]
        down = [(j, i) for i, j in up]
        last = lax.slice_in_dim(array, length - width, length, axis=dim)
        leading = lax.slice_in_dim(array, 0, width, axis=dim)
        before = lax.ppermute(last, axis, up)
        after = lax.ppermute(leading, axis, down)
        array = jnp.concatenate([before, array, after], axis=dim)
    return array


def pad_cycle(stacked):
    wide = with_halo(stacked, (("lon", 3),), 1, True)
    return with_halo(wide, (("lat", 2),), 1, False)


def conv_taps(padded, kernel, flipped):
    band_rows = padded.shape[1] - 2
    band_cols = padded.shape[2] - 2
    total = jnp.zeros((padded.shape[0], band_rows, band_cols, kernel.shape[2]), F32)
    for row_off in range(3):
        for col_off in range(3):
            window = padded[:, row_off : row_off + band_rows, col_off : col_off + band_cols, :]
            tap = 3 * row_off + col_off
            total = total + jnp.einsum(
                "bijd,cd->bijc" if flipped else "bijc,cd->bijd",
                window,
                kernel[8 - tap if flipped else tap],
                preferred_element_type=F32,
            )
    return total


def kernel_terms(padded, grad_field):
    band_rows = grad_field.shape[1]
    band_cols = grad_field.shape[2]
    result = []
    for row_off in range(3):
        for col_off in range(3):
            window = padded[:, row_off : row_off + band_rows, col_off : col_off + band_cols, :]
            result.append(jnp.einsum("bijc,bijd->cd", window, grad_field, preferred_element_type=F32))
    return jnp.stack(result)


def general_body(state, upstream, first_kernel, second_kernel):
    scale_factor = 1.0 / math.sqrt(
        state.shape[1] * lax.axis_size("lat") * state.shape[2] * lax.axis_size("lon")
    )
    both_pad = pad_cycle(jnp.stack([state, upstream]))
    pre = conv_taps(both_pad[0], first_kernel, False)
    active = jax.nn.silu(pre).astype(BF16)
    back_act = conv_taps(both_pad[1], second_kernel, True)
    sigma = jax.nn.sigmoid(pre)
    back_pre = (back_act * sigma * (1.0 + pre * (1.0 - sigma))).astype(BF16)
    inner_pad = pad_cycle(jnp.stack([active, back_pre]))
    output_state = (state.astype(F32) + conv_taps(inner_pad[0], second_kernel, False)).astype(BF16)
    state_grad = (upstream.astype(F32) + conv_taps(inner_pad[1], first_kernel, True)).astype(BF16)
    summed = []
    for terms in (kernel_terms(both_pad[0], back_pre), kernel_terms(inner_pad[0], upstream)):
        part = lax.psum_scatter(terms, "lat", scatter_dimension=1, tiled=True)
        part = lax.psum_scatter(part, "lon", scatter_dimension=2, tiled=True)
        summed.append(part * scale_factor)
    return (output_state, state_grad, summed[0], summed[1])


def stage_plan(lat_size, chans, first):
    bits = lat_size.bit_length() - 1
    turns = [["lon"], [1], list(range(2, bits))]
    order = [0]
    for turn in (turns, turns[1:] + turns[:1], turns[2:] + turns[:2])[first]:
        order += turn
    left, plan, cols = list(range(bits)), [], chans
    for op in order:
        if op == "lon":
            plan.append((op, 2 ** len(left), 1, cols))
            cols //= 2
        else:
            at = left.index(op)
            plan.append((op, 2 ** (len(left) - 1 - at), 2**at, cols))
            left.remove(op)
    return plan


PIECES = (((2, 0), (1, 0)), ((2, 1), (1, 1)), ((2, 2), (1, 2)))
ORDER = ((0, 0), (1, 0), (2, 0), (0, 1), (1, 1), (2, 1))


def fused_kernel(lat_size, scale, plans, names, *refs):
    r = dict(zip(names, refs))
    z = r["z"]
    batch, padded_rows, cols = z.shape[1], z.shape[2], z.shape[3]
    rows = padded_rows - 2
    chans = z.shape[4] // 3
    mid = slice(chans, 2 * chans)
    n_stage = 2 * padded_rows
    lat, lon = lax.axis_index("lat"), lax.axis_index("lon")
    other_lon = 1 - lon
    bits = lat_size.bit_length() - 1

    def bit_of(k):
        return lax.rem(lax.div(lat, 2**k), 2)

    def partner(k):
        return lat + (1 - 2 * bit_of(k)) * 2**k

    loads = [
        pltpu.make_async_copy(r["state"], z.at[0, :, 1 : rows + 1, :, mid], r["load_sem"].at[0]),
        pltpu.make_async_copy(r["upstream"], z.at[1, :, 1 : rows + 1, :, mid], r["load_sem"].at[1]),
        pltpu.make_async_copy(r["k1"], r["w1"], r["load_sem"].at[2]),
        pltpu.make_async_copy(r["k2"], r["w2"], r["load_sem"].at[3]),
    ]
    for load in loads:
        load.start()

    barrier = pltpu.get_barrier_semaphore()

    def greet(to_lat, to_lon):
        pl.semaphore_signal(barrier, inc=1, device_id=(to_lat, to_lon), device_id_type=MESH)

    greet(lat, other_lon)
    for k in range(1, bits):
        greet(partner(k), lon)

    @pl.when(lat > 0)
    def _():
        greet(lat - 1, lon)
        greet(lat - 1, other_lon)

    @pl.when(lat < lat_size - 1)
    def _():
        greet(lat + 1, lon)
        greet(lat + 1, other_lon)

    beside = jnp.where(lat > 0, 2, 0) + jnp.where(lat < lat_size - 1, 2, 0)
    pl.semaphore_wait(barrier, bits + beside)

    def row_copy(pair, f, up):
        src, dst = (rows, 0) if up else (1, rows + 1)
        return pltpu.make_async_remote_copy(
            src_ref=z.at[2 * pair + f, :, src, :, mid],
            dst_ref=z.at[2 * pair + f, :, dst, :, mid],
            send_sem=r["row_send"].at[pair, f, int(up)],
            recv_sem=r["row_recv"].at[pair, f, int(up)],
            device_id=(lat + 1 if up else lat - 1, lon),
            device_id_type=MESH,
        )

    def rim_copy(pair):
        return pltpu.make_async_remote_copy(
            src_ref=r["rim_out"].at[pair],
            dst_ref=r["rim_in"].at[pair],
            send_sem=r["rim_send"].at[pair],
            recv_sem=r["rim_recv"].at[pair],
            device_id=(lat, other_lon),
            device_id_type=MESH,
        )

    def corner_copy(pair, up):
        return pltpu.make_async_remote_copy(
            src_ref=r["corner_out"].at[pair, int(up)],
            dst_ref=r["corner_in"].at[pair, int(up)],
            send_sem=r["corner_send"].at[pair, int(up)],
            recv_sem=r["corner_recv"].at[pair, int(up)],
            device_id=(lat + 1 if up else lat - 1, other_lon),
            device_id_type=MESH,
        )

    def both_ways(up_copies, down_copies, what, mirrored):
        @pl.when(lat < lat_size - 1)
        def _():
            for c in down_copies if mirrored else up_copies:
                getattr(c, what)()

        @pl.when(lat > 0)
        def _():
            for c in up_copies if mirrored else down_copies:
                getattr(c, what)()

    def copies(pair):
        ups = [corner_copy(pair, True)] + [row_copy(pair, f, True) for f in range(2)]
        downs = [corner_copy(pair, False)] + [row_copy(pair, f, False) for f in range(2)]
        return ups, downs, [rim_copy(pair)]

    def send_halo(pair):
        ups, downs, flats = copies(pair)
        both_ways(ups[1:], downs[1:], "start", False)
        for f in range(2):
            for side, lo, pick in ((1, 0, 0), (0, cols - 16, 15)):
                for b in range(batch):
                    for i in range(1, rows + 1):
                        block = z[2 * pair + f, b, i, lo : lo + 16, mid].astype(F32)
                        r["rim32"][f, side, 2 * i + b : 2 * i + b + 1, :] = block[pick : pick + 1]
        for f in range(2):
            for side in range(2):
                r["rim_out"][pair, side, f] = r["rim32"][f, side].astype(BF16)
                k = 2 * (2 * side + f)
                r["corner32"][0, k : k + 2] = r["rim32"][f, side, 2:4]
                r["corner32"][1, k : k + 2] = r["rim32"][f, side, n_stage - 4 : n_stage - 2]
        for up in range(2):
            r["corner_out"][pair, up] = r["corner32"][up].astype(BF16)
        for c in flats:
            c.start()
        both_ways(ups[:1], downs[:1], "start", False)

    def shift_rows(pair, row_list):
        for f in range(2):
            fld = 2 * pair + f
            for b in range(batch):
                for i in row_list:
                    x = z[fld, b, i, :, mid].astype(F32)
                    z[fld, b, i, :, 0:chans] = pltpu.roll(x, 1, 0).astype(BF16)
                    z[fld, b, i, :, 2 * chans :] = pltpu.roll(x, cols - 1, 0).astype(BF16)

    def receive_halo(pair):
        ups, downs, flats = copies(pair)
        for c in flats:
            c.wait_recv()
        both_ways(ups, downs, "wait_recv", True)
        zero_row = jnp.zeros((batch, cols, chans), BF16)

        @pl.when(lat == 0)
        def _():
            r["corner_in"][pair, 1] = jnp.zeros((16, chans), BF16)
            for f in range(2):
                z[2 * pair + f, :, 0, :, mid] = zero_row

        @pl.when(lat == lat_size - 1)
        def _():
            r["corner_in"][pair, 0] = jnp.zeros((16, chans), BF16)
            for f in range(2):
                z[2 * pair + f, :, rows + 1, :, mid] = zero_row

        for up in range(2):
            r["corner32"][up] = r["corner_in"][pair, up].astype(F32)
        for f in range(2):
            for s in range(2):
                k = 2 * (2 * s + f)
                r["rim32"][f, s] = r["rim_in"][pair, s, f].astype(F32)
                r["rim32"][f, s, 0:2] = r["corner32"][1, k : k + 2]
                r["rim32"][f, s, n_stage - 2 :] = r["corner32"][0, k : k + 2]
        shift_rows(pair, (0, rows + 1))
        first = lax.broadcasted_iota(jnp.int32, (16, chans), 0) == 0
        final = lax.broadcasted_iota(jnp.int32, (16, chans), 0) == 15
        for f in range(2):
            fld = 2 * pair + f
            for b in range(batch):
                for i in range(padded_rows):
                    k = 2 * i + b
                    old = z[fld, b, i, 0:16, 0:chans].astype(F32)
                    z[fld, b, i, 0:16, 0:chans] = jnp.where(first, r["rim32"][f, 0, k : k + 1], old).astype(BF16)
                    old = z[fld, b, i, cols - 16 :, 2 * chans :].astype(F32)
                    z[fld, b, i, cols - 16 :, 2 * chans :] = jnp.where(
                        final, r["rim32"][f, 1, k : k + 1], old
                    ).astype(BF16)

    def finish_halo(pair):
        ups, downs, flats = copies(pair)
        for c in flats:
            c.wait_send()
        both_ways(ups, downs, "wait_send", False)

    def stage_copy(grp, s, p):
        op = plans[grp][s][0]
        to = (lat, other_lon) if op == "lon" else (partner(op), lon)
        return pltpu.make_async_remote_copy(
            src_ref=r[f"send{grp}{s}"].at[p],
            dst_ref=r[f"recv{grp}{s}"].at[p],
            send_sem=r["rs_send"].at[grp, s, p],
            recv_sem=r["rs_recv"].at[grp, s, p],
            device_id=to,
            device_id_type=MESH,
        )

    def half(grp, s, p, mine):
        op, _, _, width = plans[grp][s]
        keep = r[f"keep{grp}{s}"]
        if op == "lon":
            start = pl.multiple_of((lon if mine else other_lon) * (width // 2), width // 2)
            return keep[p, :, :, :, :, pl.ds(start, width // 2)]
        which = bit_of(op) if mine else 1 - bit_of(op)
        return keep[p, :, :, which]

    def put(grp, s, p, value):
        keep = r[f"keep{grp}{s}"]
        keep[p] = value.reshape(keep.shape[1:])
        r[f"send{grp}{s}"][p] = half(grp, s, p, False).astype(BF16)
        stage_copy(grp, s, p).start()

    def advance(grp, s, p):
        stage_copy(grp, s, p).wait_recv()
        value = half(grp, s, p, True) + r[f"recv{grp}{s}"][p].astype(F32)
        if s + 1 < len(plans[grp]):
            put(grp, s + 1, p, value)
            return
        value = (value * scale).reshape(3, value.shape[-2], value.shape[-1])
        grad, e = PIECES[grp][p]
        if grad == 2:
            for f in range(3):
                r["g2"][8 - 3 * e - f] = value[f]
        else:
            r["g1"][3 * e : 3 * e + 3] = value

    def window(fld, e):
        return z[fld, :, e : e + rows].reshape(batch * rows * cols, 3 * chans)

    def conv(fld, w, b):
        total = None
        for e in range(3):
            x = z[fld, b, e : e + rows].reshape(rows * cols, 3 * chans)
            part = jnp.dot(x, w[3 * e : 3 * e + 3].reshape(3 * chans, chans), preferred_element_type=F32)
            total = part if total is None else total + part
        return total

    loads[0].wait()
    loads[1].wait()
    send_halo(0)
    shift_rows(0, range(1, rows + 1))
    loads[2].wait()
    loads[3].wait()
    for t in range(9):
        r["w2t"][8 - t] = r["w2"][t].T
    receive_halo(0)

    for b in range(batch):
        pre = conv(0, r["w1"], b)
        sigma = 1.0 / (1.0 + jnp.exp(-pre))
        active = (pre * sigma).astype(BF16)
        z[2, b, 1 : rows + 1, :, mid] = active.reshape(rows, cols, chans)
        r["slope"][b] = sigma * (1.0 + pre * (1.0 - sigma))
    act = z[2, :, 1 : rows + 1, :, mid].reshape(batch * rows * cols, chans)
    for e in range(3):
        terms = lax.dot_general(act, window(1, e), (((0,), (0,)), ((), ())), preferred_element_type=F32)
        grp, p = ORDER[e]
        put(grp, 0, p, jnp.stack([terms[:, f * chans : (f + 1) * chans] for f in range(3)]))
    early, late = ORDER[:3], ORDER[3:]

    def advance_all(s, pieces):
        for grp, p in pieces:
            advance(grp, s, p)

    for b in range(batch):
        back = (conv(1, r["w2t"], b) * r["slope"][b]).astype(BF16)
        z[3, b, 1 : rows + 1, :, mid] = back.reshape(rows, cols, chans)
        if b == 0:
            advance_all(0, early)
    back = z[3, :, 1 : rows + 1, :, mid].reshape(batch * rows * cols, chans)
    for e in range(3):
        terms = lax.dot_general(window(0, e), back, (((0,), (0,)), ((), ())), preferred_element_type=F32)
        grp, p = late[e]
        put(grp, 0, p, terms)
    send_halo(1)
    advance_all(0, late)
    advance_all(1, early)
    shift_rows(1, range(1, rows + 1))
    for t in range(9):
        r["w1t"][8 - t] = r["w1"][t].T
    advance_all(1, late)
    receive_halo(1)
    advance_all(2, early)

    def finish_field(fld, w, name, b):
        near = z[fld, b, 1 : rows + 1, :, mid].astype(F32)
        r[name][b] = (near + conv(fld + 2, w, b).reshape(rows, cols, chans)).astype(BF16)

    finish_field(0, r["w2"], "out", 0)
    advance_all(2, late)
    finish_field(0, r["w2"], "out", 1)
    advance_all(3, early)
    finish_field(1, r["w1t"], "sgrad", 0)
    advance_all(3, late)
    finish_field(1, r["w1t"], "sgrad", 1)
    for s in range(4, len(plans[0])):
        advance_all(s, early)
        advance_all(s, late)
    for pair in range(2):
        finish_halo(pair)
    for grp in range(3):
        for s in range(len(plans[grp])):
            for p in range(2):
                stage_copy(grp, s, p).wait_send()


def fused_body(state, upstream, first_kernel, second_kernel):
    lat_size, lon_size = lax.axis_size("lat"), lax.axis_size("lon")
    batch, rows, cols, chans = state.shape
    scale = 1.0 / math.sqrt(rows * lat_size * cols * lon_size)
    own = chans // lat_size
    n_stage = 2 * (rows + 2)
    plans = [stage_plan(lat_size, chans, first) for first in range(3)]
    steps = len(plans[0])
    scratch = {
        "z": pltpu.VMEM((4, batch, rows + 2, cols, 3 * chans), BF16),
        "w1": pltpu.VMEM((9, chans, chans), BF16),
        "w2": pltpu.VMEM((9, chans, chans), BF16),
        "w1t": pltpu.VMEM((9, chans, chans), BF16),
        "w2t": pltpu.VMEM((9, chans, chans), BF16),
        "slope": pltpu.VMEM((batch, rows * cols, chans), F32),
        "rim32": pltpu.VMEM((2, 2, n_stage, chans), F32),
        "rim_out": pltpu.VMEM((2, 2, 2, n_stage, chans), BF16),
        "rim_in": pltpu.VMEM((2, 2, 2, n_stage, chans), BF16),
        "corner32": pltpu.VMEM((2, 16, chans), F32),
        "corner_out": pltpu.VMEM((2, 2, 16, chans), BF16),
        "corner_in": pltpu.VMEM((2, 2, 16, chans), BF16),
        "load_sem": pltpu.SemaphoreType.DMA((4,)),
        "row_send": pltpu.SemaphoreType.DMA((2, 2, 2)),
        "row_recv": pltpu.SemaphoreType.DMA((2, 2, 2)),
        "rim_send": pltpu.SemaphoreType.DMA((2,)),
        "rim_recv": pltpu.SemaphoreType.DMA((2,)),
        "corner_send": pltpu.SemaphoreType.DMA((2, 2)),
        "corner_recv": pltpu.SemaphoreType.DMA((2, 2)),
        "rs_send": pltpu.SemaphoreType.DMA((3, steps, 2)),
        "rs_recv": pltpu.SemaphoreType.DMA((3, steps, 2)),
    }
    for grp in range(3):
        for s, (op, high, low, width) in enumerate(plans[grp]):
            if op == "lon":
                kept, sent = (2, 3, high, low, own, width), (2, 3, high, low, own, width // 2)
            else:
                kept, sent = (2, 3, high, 2, low, own, width), (2, 3, high, low, own, width)
            scratch[f"keep{grp}{s}"] = pltpu.VMEM(kept, F32)
            scratch[f"send{grp}{s}"] = pltpu.VMEM(sent, BF16)
            scratch[f"recv{grp}{s}"] = pltpu.VMEM(sent, BF16)
    names = ["state", "upstream", "k1", "k2", "out", "sgrad", "g1", "g2"] + list(scratch)

    def kernel(*refs):
        fused_kernel(lat_size, scale, plans, names, *refs)

    vmem = pl.BlockSpec(memory_space=pltpu.VMEM)
    anywhere = pl.BlockSpec(memory_space=pltpu.HBM)
    kinds = [(state.shape, BF16)] * 2 + [((9, own, chans // 2), F32)] * 2
    held = pl.pallas_call(
        kernel,
        out_shape=tuple(pltpu.VMEM(shape, kind) for shape, kind in kinds),
        in_specs=[anywhere] * 4,
        out_specs=(vmem,) * 4,
        scratch_shapes=list(scratch.values()),
        compiler_params=pltpu.CompilerParams(
            collective_id=0, has_side_effects=True, vmem_limit_bytes=56 * 2**20
        ),
    )(*[pltpu.with_memory_space_constraint(x, pltpu.HBM) for x in (state, upstream, first_kernel, second_kernel)])

    def write_out(*refs):
        moves = [pltpu.make_async_copy(refs[i], refs[4 + i], refs[8].at[i]) for i in range(4)]
        for move in moves:
            move.start()
        for move in moves:
            move.wait()

    return pl.pallas_call(
        write_out,
        out_shape=tuple(jax.ShapeDtypeStruct(shape, kind) for shape, kind in kinds),
        in_specs=[vmem] * 4,
        out_specs=(anywhere,) * 4,
        scratch_shapes=[pltpu.SemaphoreType.DMA((4,))],
    )(*[pltpu.with_memory_space_constraint(h, pltpu.VMEM) for h in held])


def body(state, upstream, first_kernel, second_kernel):
    lat_size, lon_size = lax.axis_size("lat"), lax.axis_size("lon")
    batch, rows, cols, chans = state.shape
    fits = (
        lon_size == 2
        and lat_size >= 16
        and lat_size & (lat_size - 1) == 0
        and batch == 2
        and 2 * (rows + 2) == 16
        and cols % 16 == 0
        and chans % (16 * lat_size) == 0
        and (chans // 2) % 128 == 0
    )
    run = fused_body if fits else general_body
    return run(state, upstream, first_kernel, second_kernel)


def solution(mesh):
    placed = (P(None, "lat", "lon", None), P(None, "lat", "lon", None), P(), P())
    return jax.shard_map(
        body,
        mesh=mesh,
        in_specs=placed,
        out_specs=(
            P(None, "lat", "lon", None),
            P(None, "lat", "lon", None),
            P(None, "lat", "lon"),
            P(None, "lat", "lon"),
        ),
        check_vma=False,
    )
```

```python
import math

import jax
import jax.numpy as jnp
from jax import lax
from jax.experimental import pallas as pl
from jax.experimental.pallas import tpu as pltpu
from jax.sharding import PartitionSpec as P

F32 = jnp.float32
BF16 = jnp.bfloat16
MESH = pl.DeviceIdType.MESH


def with_halo(array, sides, width, wrap):
    for axis, dim in sides:
        size, length = (lax.axis_size(axis), array.shape[dim])
        up = [(i, (i + 1) % size) for i in range(size if wrap else size - 1)]
        down = [(j, i) for i, j in up]
        last = lax.slice_in_dim(array, length - width, length, axis=dim)
        leading = lax.slice_in_dim(array, 0, width, axis=dim)
        before = lax.ppermute(last, axis, up)
        after = lax.ppermute(leading, axis, down)
        array = jnp.concatenate([before, array, after], axis=dim)
    return array


def pad_cycle(stacked):
    wide = with_halo(stacked, (("lon", 3),), 1, True)
    return with_halo(wide, (("lat", 2),), 1, False)


def conv_taps(padded, kernel, flipped):
    band_rows = padded.shape[1] - 2
    band_cols = padded.shape[2] - 2
    total = jnp.zeros((padded.shape[0], band_rows, band_cols, kernel.shape[2]), F32)
    for row_off in range(3):
        for col_off in range(3):
            window = padded[:, row_off : row_off + band_rows, col_off : col_off + band_cols, :]
            tap = 3 * row_off + col_off
            total = total + jnp.einsum(
                "bijd,cd->bijc" if flipped else "bijc,cd->bijd",
                window,
                kernel[8 - tap if flipped else tap],
                preferred_element_type=F32,
            )
    return total


def kernel_terms(padded, grad_field):
    band_rows = grad_field.shape[1]
    band_cols = grad_field.shape[2]
    result = []
    for row_off in range(3):
        for col_off in range(3):
            window = padded[:, row_off : row_off + band_rows, col_off : col_off + band_cols, :]
            result.append(jnp.einsum("bijc,bijd->cd", window, grad_field, preferred_element_type=F32))
    return jnp.stack(result)


def general_body(state, upstream, first_kernel, second_kernel):
    scale_factor = 1.0 / math.sqrt(
        state.shape[1] * lax.axis_size("lat") * state.shape[2] * lax.axis_size("lon")
    )
    both_pad = pad_cycle(jnp.stack([state, upstream]))
    pre = conv_taps(both_pad[0], first_kernel, False)
    active = jax.nn.silu(pre).astype(BF16)
    back_act = conv_taps(both_pad[1], second_kernel, True)
    sigma = jax.nn.sigmoid(pre)
    back_pre = (back_act * sigma * (1.0 + pre * (1.0 - sigma))).astype(BF16)
    inner_pad = pad_cycle(jnp.stack([active, back_pre]))
    output_state = (state.astype(F32) + conv_taps(inner_pad[0], second_kernel, False)).astype(BF16)
    state_grad = (upstream.astype(F32) + conv_taps(inner_pad[1], first_kernel, True)).astype(BF16)
    summed = []
    for terms in (kernel_terms(both_pad[0], back_pre), kernel_terms(inner_pad[0], upstream)):
        part = lax.psum_scatter(terms, "lat", scatter_dimension=1, tiled=True)
        part = lax.psum_scatter(part, "lon", scatter_dimension=2, tiled=True)
        summed.append(part * scale_factor)
    return (output_state, state_grad, summed[0], summed[1])


def stage_plan(lat_size, chans, lon_first):
    bits = lat_size.bit_length() - 1
    order = [0, "lon", 1] if lon_first else [0, 1, "lon"]
    order += list(range(2, bits))
    plan, length, cols = [], lat_size, chans
    for op in order:
        plan.append((op, length, cols))
        if op == "lon":
            cols //= 2
        else:
            length //= 2
    return plan


PIECES = (((2, 0), (2, 2), (1, 1)), ((2, 1), (1, 0), (1, 2)))
ORDER = ((0, 0), (1, 0), (0, 1), (1, 1), (0, 2), (1, 2))


def fused_kernel(lat_size, scale, plans, names, *refs):
    r = dict(zip(names, refs))
    z = r["z"]
    batch, padded_rows, cols = z.shape[1], z.shape[2], z.shape[3]
    rows = padded_rows - 2
    chans = z.shape[4] // 3
    mid = slice(chans, 2 * chans)
    n_stage = 2 * padded_rows
    lat, lon = lax.axis_index("lat"), lax.axis_index("lon")
    other_lon = 1 - lon
    bits = lat_size.bit_length() - 1

    def bit_of(k):
        return lax.rem(lax.div(lat, 2**k), 2)

    def partner(k):
        return lat + (1 - 2 * bit_of(k)) * 2**k

    loads = [
        pltpu.make_async_copy(r["state"], z.at[0, :, 1 : rows + 1, :, mid], r["load_sem"].at[0]),
        pltpu.make_async_copy(r["upstream"], z.at[1, :, 1 : rows + 1, :, mid], r["load_sem"].at[1]),
        pltpu.make_async_copy(r["k1"], r["w1"], r["load_sem"].at[2]),
        pltpu.make_async_copy(r["k2"], r["w2"], r["load_sem"].at[3]),
    ]
    for load in loads:
        load.start()

    barrier = pltpu.get_barrier_semaphore()

    def greet(to_lat, to_lon):
        pl.semaphore_signal(barrier, inc=1, device_id=(to_lat, to_lon), device_id_type=MESH)

    greet(lat, other_lon)
    for k in range(1, bits):
        greet(partner(k), lon)

    @pl.when(lat > 0)
    def _():
        greet(lat - 1, lon)
        greet(lat - 1, other_lon)

    @pl.when(lat < lat_size - 1)
    def _():
        greet(lat + 1, lon)
        greet(lat + 1, other_lon)

    beside = jnp.where(lat > 0, 2, 0) + jnp.where(lat < lat_size - 1, 2, 0)
    pl.semaphore_wait(barrier, bits + beside)

    def row_copy(pair, f, up):
        src, dst = (rows, 0) if up else (1, rows + 1)
        return pltpu.make_async_remote_copy(
            src_ref=z.at[2 * pair + f, :, src, :, mid],
            dst_ref=z.at[2 * pair + f, :, dst, :, mid],
            send_sem=r["row_send"].at[pair, f, int(up)],
            recv_sem=r["row_recv"].at[pair, f, int(up)],
            device_id=(lat + 1 if up else lat - 1, lon),
            device_id_type=MESH,
        )

    def rim_copy(pair):
        return pltpu.make_async_remote_copy(
            src_ref=r["rim_out"].at[pair],
            dst_ref=r["rim_in"].at[pair],
            send_sem=r["rim_send"].at[pair],
            recv_sem=r["rim_recv"].at[pair],
            device_id=(lat, other_lon),
            device_id_type=MESH,
        )

    def corner_copy(pair, up):
        return pltpu.make_async_remote_copy(
            src_ref=r["corner_out"].at[pair, int(up)],
            dst_ref=r["corner_in"].at[pair, int(up)],
            send_sem=r["corner_send"].at[pair, int(up)],
            recv_sem=r["corner_recv"].at[pair, int(up)],
            device_id=(lat + 1 if up else lat - 1, other_lon),
            device_id_type=MESH,
        )

    def both_ways(up_copies, down_copies, what, mirrored):
        @pl.when(lat < lat_size - 1)
        def _():
            for c in down_copies if mirrored else up_copies:
                getattr(c, what)()

        @pl.when(lat > 0)
        def _():
            for c in up_copies if mirrored else down_copies:
                getattr(c, what)()

    def copies(pair):
        ups = [corner_copy(pair, True)] + [row_copy(pair, f, True) for f in range(2)]
        downs = [corner_copy(pair, False)] + [row_copy(pair, f, False) for f in range(2)]
        return ups, downs, [rim_copy(pair)]

    def send_halo(pair):
        for f in range(2):
            for side, lo, pick in ((1, 0, 0), (0, cols - 16, 15)):
                for b in range(batch):
                    for i in range(1, rows + 1):
                        block = z[2 * pair + f, b, i, lo : lo + 16, mid].astype(F32)
                        r["rim32"][f, side, 2 * i + b : 2 * i + b + 1, :] = block[pick : pick + 1]
        for f in range(2):
            for side in range(2):
                r["rim_out"][pair, side, f] = r["rim32"][f, side].astype(BF16)
                k = 2 * (2 * side + f)
                r["corner32"][0, k : k + 2] = r["rim32"][f, side, 2:4]
                r["corner32"][1, k : k + 2] = r["rim32"][f, side, n_stage - 4 : n_stage - 2]
        for up in range(2):
            r["corner_out"][pair, up] = r["corner32"][up].astype(BF16)
        ups, downs, flats = copies(pair)
        for c in flats:
            c.start()
        both_ways(ups, downs, "start", False)

    def shift_rows(pair, row_list):
        for f in range(2):
            fld = 2 * pair + f
            for b in range(batch):
                for i in row_list:
                    x = z[fld, b, i, :, mid].astype(F32)
                    z[fld, b, i, :, 0:chans] = pltpu.roll(x, 1, 0).astype(BF16)
                    z[fld, b, i, :, 2 * chans :] = pltpu.roll(x, cols - 1, 0).astype(BF16)

    def receive_halo(pair):
        ups, downs, flats = copies(pair)
        for c in flats:
            c.wait_recv()
        both_ways(ups, downs, "wait_recv", True)
        zero_row = jnp.zeros((batch, cols, chans), BF16)

        @pl.when(lat == 0)
        def _():
            r["corner_in"][pair, 1] = jnp.zeros((16, chans), BF16)
            for f in range(2):
                z[2 * pair + f, :, 0, :, mid] = zero_row

        @pl.when(lat == lat_size - 1)
        def _():
            r["corner_in"][pair, 0] = jnp.zeros((16, chans), BF16)
            for f in range(2):
                z[2 * pair + f, :, rows + 1, :, mid] = zero_row

        for up in range(2):
            r["corner32"][up] = r["corner_in"][pair, up].astype(F32)
        for f in range(2):
            for s in range(2):
                k = 2 * (2 * s + f)
                r["rim32"][f, s] = r["rim_in"][pair, s, f].astype(F32)
                r["rim32"][f, s, 0:2] = r["corner32"][1, k : k + 2]
                r["rim32"][f, s, n_stage - 2 :] = r["corner32"][0, k : k + 2]
        shift_rows(pair, (0, rows + 1))
        first = lax.broadcasted_iota(jnp.int32, (16, chans), 0) == 0
        final = lax.broadcasted_iota(jnp.int32, (16, chans), 0) == 15
        for f in range(2):
            fld = 2 * pair + f
            for b in range(batch):
                for i in range(padded_rows):
                    k = 2 * i + b
                    old = z[fld, b, i, 0:16, 0:chans].astype(F32)
                    z[fld, b, i, 0:16, 0:chans] = jnp.where(first, r["rim32"][f, 0, k : k + 1], old).astype(BF16)
                    old = z[fld, b, i, cols - 16 :, 2 * chans :].astype(F32)
                    z[fld, b, i, cols - 16 :, 2 * chans :] = jnp.where(
                        final, r["rim32"][f, 1, k : k + 1], old
                    ).astype(BF16)

    def finish_halo(pair):
        ups, downs, flats = copies(pair)
        for c in flats:
            c.wait_send()
        both_ways(ups, downs, "wait_send", False)

    def stage_copy(grp, s, p):
        op = plans[grp][s][0]
        to = (lat, other_lon) if op == "lon" else (partner(op), lon)
        return pltpu.make_async_remote_copy(
            src_ref=r[f"send{grp}{s}"].at[p],
            dst_ref=r[f"recv{grp}{s}"].at[p],
            send_sem=r["rs_send"].at[grp, s, p],
            recv_sem=r["rs_recv"].at[grp, s, p],
            device_id=to,
            device_id_type=MESH,
        )

    def half(grp, s, p, mine):
        op, length, width = plans[grp][s]
        keep = r[f"keep{grp}{s}"]
        if op == "lon":
            start = pl.multiple_of((lon if mine else other_lon) * (width // 2), width // 2)
            return keep[p, :, :, :, pl.ds(start, width // 2)]
        which = bit_of(op) if mine else 1 - bit_of(op)
        return keep[p, :, :, which]

    def put(grp, s, p, value):
        keep = r[f"keep{grp}{s}"]
        keep[p] = value.reshape(keep.shape[1:])
        r[f"send{grp}{s}"][p] = half(grp, s, p, False).astype(BF16)
        stage_copy(grp, s, p).start()

    def advance(grp, s, p):
        stage_copy(grp, s, p).wait_recv()
        value = half(grp, s, p, True) + r[f"recv{grp}{s}"][p].astype(F32)
        if s + 1 < len(plans[grp]):
            put(grp, s + 1, p, value)
            return
        value = (value * scale).reshape(3, value.shape[2], value.shape[3])
        grad, e = PIECES[grp][p]
        if grad == 2:
            for f in range(3):
                r["g2"][8 - 3 * e - f] = value[f]
        else:
            r["g1"][3 * e : 3 * e + 3] = value

    def window(fld, e):
        return z[fld, :, e : e + rows].reshape(batch * rows * cols, 3 * chans)

    def conv(fld, w, b):
        total = None
        for e in range(3):
            x = z[fld, b, e : e + rows].reshape(rows * cols, 3 * chans)
            part = jnp.dot(x, w[3 * e : 3 * e + 3].reshape(3 * chans, chans), preferred_element_type=F32)
            total = part if total is None else total + part
        return total

    loads[0].wait()
    loads[1].wait()
    send_halo(0)
    shift_rows(0, range(1, rows + 1))
    loads[2].wait()
    loads[3].wait()
    for t in range(9):
        r["w1t"][8 - t] = r["w1"][t].T
        r["w2t"][8 - t] = r["w2"][t].T
    receive_halo(0)

    for b in range(batch):
        pre = conv(0, r["w1"], b)
        sigma = 1.0 / (1.0 + jnp.exp(-pre))
        active = (pre * sigma).astype(BF16)
        z[2, b, 1 : rows + 1, :, mid] = active.reshape(rows, cols, chans)
        r["slope"][b] = sigma * (1.0 + pre * (1.0 - sigma))
    act = z[2, :, 1 : rows + 1, :, mid].reshape(batch * rows * cols, chans)
    for e in range(3):
        terms = lax.dot_general(act, window(1, e), (((0,), (0,)), ((), ())), preferred_element_type=F32)
        grp, p = ORDER[e]
        put(grp, 0, p, jnp.stack([terms[:, f * chans : (f + 1) * chans] for f in range(3)]))
    for b in range(batch):
        back = (conv(1, r["w2t"], b) * r["slope"][b]).astype(BF16)
        z[3, b, 1 : rows + 1, :, mid] = back.reshape(rows, cols, chans)
    send_halo(1)

    def advance_all(s, pieces):
        for grp, p in pieces:
            advance(grp, s, p)

    early, late = ORDER[:3], ORDER[3:]
    advance_all(0, early)
    back = z[3, :, 1 : rows + 1, :, mid].reshape(batch * rows * cols, chans)
    for e in range(3):
        terms = lax.dot_general(window(0, e), back, (((0,), (0,)), ((), ())), preferred_element_type=F32)
        grp, p = late[e]
        put(grp, 0, p, terms)
    advance_all(0, late)
    advance_all(1, early)
    shift_rows(1, range(1, rows + 1))
    receive_halo(1)

    def finish_field(fld, w, name, b):
        near = z[fld, b, 1 : rows + 1, :, mid].astype(F32)
        r[name][b] = (near + conv(fld + 2, w, b).reshape(rows, cols, chans)).astype(BF16)

    finish_field(0, r["w2"], "out", 0)
    advance_all(1, late)
    finish_field(0, r["w2"], "out", 1)
    advance_all(2, early)
    finish_field(1, r["w1t"], "sgrad", 0)
    advance_all(2, late)
    finish_field(1, r["w1t"], "sgrad", 1)
    for s in range(3, len(plans[0])):
        advance_all(s, early)
        advance_all(s, late)
    for pair in range(2):
        finish_halo(pair)
    for grp in range(2):
        for s in range(len(plans[grp])):
            for e in range(3):
                stage_copy(grp, s, e).wait_send()


def fused_body(state, upstream, first_kernel, second_kernel):
    lat_size, lon_size = lax.axis_size("lat"), lax.axis_size("lon")
    batch, rows, cols, chans = state.shape
    scale = 1.0 / math.sqrt(rows * lat_size * cols * lon_size)
    own = chans // lat_size
    n_stage = 2 * (rows + 2)
    plans = [stage_plan(lat_size, chans, True), stage_plan(lat_size, chans, False)]
    steps = len(plans[0])
    scratch = {
        "z": pltpu.VMEM((4, batch, rows + 2, cols, 3 * chans), BF16),
        "w1": pltpu.VMEM((9, chans, chans), BF16),
        "w2": pltpu.VMEM((9, chans, chans), BF16),
        "w1t": pltpu.VMEM((9, chans, chans), BF16),
        "w2t": pltpu.VMEM((9, chans, chans), BF16),
        "slope": pltpu.VMEM((batch, rows * cols, chans), F32),
        "rim32": pltpu.VMEM((2, 2, n_stage, chans), F32),
        "rim_out": pltpu.VMEM((2, 2, 2, n_stage, chans), BF16),
        "rim_in": pltpu.VMEM((2, 2, 2, n_stage, chans), BF16),
        "corner32": pltpu.VMEM((2, 16, chans), F32),
        "corner_out": pltpu.VMEM((2, 2, 16, chans), BF16),
        "corner_in": pltpu.VMEM((2, 2, 16, chans), BF16),
        "load_sem": pltpu.SemaphoreType.DMA((4,)),
        "row_send": pltpu.SemaphoreType.DMA((2, 2, 2)),
        "row_recv": pltpu.SemaphoreType.DMA((2, 2, 2)),
        "rim_send": pltpu.SemaphoreType.DMA((2,)),
        "rim_recv": pltpu.SemaphoreType.DMA((2,)),
        "corner_send": pltpu.SemaphoreType.DMA((2, 2)),
        "corner_recv": pltpu.SemaphoreType.DMA((2, 2)),
        "rs_send": pltpu.SemaphoreType.DMA((2, steps, 3)),
        "rs_recv": pltpu.SemaphoreType.DMA((2, steps, 3)),
    }
    for grp in range(2):
        for s, (op, length, width) in enumerate(plans[grp]):
            if op == "lon":
                kept, sent = (3, length, own, width), (3, length, own, width // 2)
            else:
                kept, sent = (3, length // 2, 2, own, width), (3, length // 2, own, width)
            scratch[f"keep{grp}{s}"] = pltpu.VMEM((3,) + kept, F32)
            scratch[f"send{grp}{s}"] = pltpu.VMEM((3,) + sent, BF16)
            scratch[f"recv{grp}{s}"] = pltpu.VMEM((3,) + sent, BF16)
    names = ["state", "upstream", "k1", "k2", "out", "sgrad", "g1", "g2"] + list(scratch)

    def kernel(*refs):
        fused_kernel(lat_size, scale, plans, names, *refs)

    vmem = pl.BlockSpec(memory_space=pltpu.VMEM)
    anywhere = pl.BlockSpec(memory_space=pltpu.HBM)
    kinds = [(state.shape, BF16)] * 2 + [((9, own, chans // 2), F32)] * 2
    held = pl.pallas_call(
        kernel,
        out_shape=tuple(pltpu.VMEM(shape, kind) for shape, kind in kinds),
        in_specs=[anywhere] * 4,
        out_specs=(vmem,) * 4,
        scratch_shapes=list(scratch.values()),
        compiler_params=pltpu.CompilerParams(
            collective_id=0, has_side_effects=True, vmem_limit_bytes=56 * 2**20
        ),
    )(*[pltpu.with_memory_space_constraint(x, pltpu.HBM) for x in (state, upstream, first_kernel, second_kernel)])

    def write_out(*refs):
        moves = [pltpu.make_async_copy(refs[i], refs[4 + i], refs[8].at[i]) for i in range(4)]
        for move in moves:
            move.start()
        for move in moves:
            move.wait()

    return pl.pallas_call(
        write_out,
        out_shape=tuple(jax.ShapeDtypeStruct(shape, kind) for shape, kind in kinds),
        in_specs=[vmem] * 4,
        out_specs=(anywhere,) * 4,
        scratch_shapes=[pltpu.SemaphoreType.DMA((4,))],
    )(*[pltpu.with_memory_space_constraint(h, pltpu.VMEM) for h in held])


def body(state, upstream, first_kernel, second_kernel):
    lat_size, lon_size = lax.axis_size("lat"), lax.axis_size("lon")
    batch, rows, cols, chans = state.shape
    fits = (
        lon_size == 2
        and lat_size >= 4
        and lat_size & (lat_size - 1) == 0
        and batch == 2
        and 2 * (rows + 2) == 16
        and cols % 16 == 0
        and chans % (16 * lat_size) == 0
        and (chans // 2) % 128 == 0
    )
    run = fused_body if fits else general_body
    return run(state, upstream, first_kernel, second_kernel)


def solution(mesh):
    placed = (P(None, "lat", "lon", None), P(None, "lat", "lon", None), P(), P())
    return jax.shard_map(
        body,
        mesh=mesh,
        in_specs=placed,
        out_specs=(
            P(None, "lat", "lon", None),
            P(None, "lat", "lon", None),
            P(None, "lat", "lon"),
            P(None, "lat", "lon"),
        ),
        check_vma=False,
    )
```
